128 devices in a mesh: lat: 32 (over z_lo, y, x), lon: 4 (over z_hi, core).
Axes of the slice: x: 4, y: 4, z: 4 (z_hi: 2, z_lo: 2; z = z_hi * 2 + z_lo), core: 2. Of those that a mesh axis runs over, the one named last changes fastest.
Arguments:
- vorticity: float32 [2, 1280, 2560], P(None, 'lat', 'lon'), may hold values from -46 to 46
- divergence: float32 [2, 1280, 2560], P(None, 'lat', 'lon'), may hold values from -46 to 46
- height: float32 [2, 1280, 2560], P(None, 'lat', 'lon'), may hold values from -46 to 46
- mean_geopot: float32 [2], replicated, may hold values from 0.5 to 8
Outputs:
- new_vorticity: float32 [2, 1280, 2560], P(None, 'lat', 'lon')
- new_divergence: float32 [2, 1280, 2560], P(None, 'lat', 'lon')
- new_height: float32 [2, 1280, 2560], P(None, 'lat', 'lon')
The draws below stay inside these ranges and needn't reach their ends.
All inputs are finite; a program needn't handle non-finite values.
Results may differ from the reference program's by a relative error of at most 0.0017.
Values sent between devices are 32-bit elements; how exact they have to be, the bound alone decides.
No kernel may reach another device: no remote copies, remote signals or barrier semaphores. Data moves between devices by JAX's collectives and lax.ppermute only.
A program may use at most 320 MiB of HBM per device.

```python
import math
import jax
import jax.numpy as jnp
from jax import lax

NLON = 2560
NLAT = 1280
MMAX = 1280
LEV = 2


amplitude = 40.0


limit = 46.0


def banded_field(base_key, field_code):
    field_key = jax.random.fold_in(base_key, field_code)
    back_key, wave_key, phase_key = jax.random.split(field_key, 3)
    shape_all = (LEV, NLAT, NLON)
    background = jnp.clip(jax.random.normal(back_key, shape_all, jnp.float32), -6.0, 6.0)
    center = 1.0
    spread = 2.0
    row_index = jnp.arange(NLAT, dtype=jnp.float32)
    colatitude = (4.0 * row_index + 3.0) * jnp.pi / (4.0 * NLAT + 2.0)
    shortfall = 1.0 / (8.0 * NLAT * NLAT) - 1.0 / (8.0 * NLAT * NLAT * NLAT)
    one_minus = shortfall + 2.0 * (1.0 - shortfall) * jnp.sin(0.5 * colatitude) ** 2
    one_plus = shortfall + 2.0 * (1.0 - shortfall) * jnp.cos(0.5 * colatitude) ** 2
    sine_rows = jnp.sqrt(one_minus * one_plus)
    offsets = jax.random.randint(wave_key, (LEV, 4), 0, max(MMAX // 16, 1), dtype=jnp.int32)
    orders = MMAX // 4 + MMAX // 8 * jnp.arange(4, dtype=jnp.int32)[None, :] + offsets
    phases = jax.random.uniform(phase_key, (LEV, 4, 2), jnp.float32, -jnp.pi, jnp.pi)
    degree_top = MMAX - 0.5
    turning = orders.astype(jnp.float32) / degree_top
    cos_turn = jnp.sqrt(1.0 - turning * turning)
    widths = cos_turn * (2.0 * degree_top * degree_top * cos_turn / turning) ** (-1.0 / 3.0)
    north_rows = jnp.arange(NLAT, dtype=jnp.int32) < NLAT // 2
    points = jnp.arange(NLON, dtype=jnp.int32)
    total = background
    for band_index in range(4):
        order_now = orders[:, band_index]
        distance = (sine_rows[None, :] - turning[:, band_index, None]) / widths[:, band_index, None]
        profile = jnp.exp(-0.5 * ((distance - center) / spread) ** 2)
        row_phase = jnp.where(north_rows[None, :], phases[:, band_index, 0:1], phases[:, band_index, 1:2])
        angle_index = order_now[:, None] * points[None, :] % NLON
        wave_angle = angle_index.astype(jnp.float32) * (2.0 * jnp.pi / NLON)
        total = total + amplitude * profile[:, :, None] * jnp.cos(wave_angle[:, None, :] + row_phase[:, :, None])
    return jnp.clip(total, -limit, limit)


def draw_vorticity(key, part):
    return banded_field(key, 11)


def draw_divergence(key, part):
    return banded_field(key, 12)


def draw_height(key, part):
    return banded_field(key, 13)


def setup_inputs(seed: int = 0) -> dict:
    key_of = jax.random.split(jax.random.key(seed), 5)
    return {
        "vorticity": draw_vorticity(jax.random.fold_in(key_of[4], 71), 0),
        "divergence": draw_divergence(jax.random.fold_in(key_of[4], 71), 0),
        "height": draw_height(jax.random.fold_in(key_of[4], 71), 0),
        "mean_geopot": jnp.clip(jnp.exp(jax.random.uniform(key_of[3], (LEV,), jnp.float32, math.log(0.5), math.log(8.0))), 0.5, 8.0),
    }


cap_sine = 0.5
filter_width = 64.0
diffusion = 4.0
renorm_big = 2.0 ** 64
renorm_step = 64.0

def latitudes(row_index):
    colatitude = (4.0 * row_index + 3.0) * jnp.pi / (4.0 * NLAT + 2.0)
    shortfall = 1.0 / (8.0 * NLAT * NLAT) - 1.0 / (8.0 * NLAT * NLAT * NLAT)
    one_minus = shortfall + 2.0 * (1.0 - shortfall) * jnp.sin(0.5 * colatitude) ** 2
    one_plus = shortfall + 2.0 * (1.0 - shortfall) * jnp.cos(0.5 * colatitude) ** 2
    return (0.5 * (one_plus - one_minus), jnp.sqrt(one_minus * one_plus))

def sector_logs(float_type):
    sector_order = jnp.arange(1, MMAX, dtype=float_type)
    log_terms = jnp.log2((2.0 * sector_order + 1.0) / (2.0 * sector_order))
    return jnp.concatenate([jnp.zeros((1,), float_type), jnp.cumsum(log_terms)])

def advance(recurrence, excess_degree, wave_col, cosine, wave_limit):
    previous, current, exponent = recurrence
    degree = wave_col + excess_degree
    first_row = excess_degree == 0
    growth = jnp.sqrt((4.0 * degree * degree - 1.0) / jnp.maximum(excess_degree * (2.0 * wave_col + excess_degree), 1.0))
    backward = jnp.sqrt(jnp.maximum((excess_degree - 1.0) * (2.0 * wave_col + excess_degree - 1.0), 0.0) / jnp.maximum(4.0 * (degree - 1.0) ** 2 - 1.0, 1.0))
    following = growth * (cosine * current - backward * previous)
    too_large = jnp.abs(following) > renorm_big
    factor = jnp.where(too_large, 1.0 / renorm_big, 1.0)
    rescaled = (current * factor, following * factor, exponent + jnp.where(too_large, renorm_step, 0.0))
    new_state = jax.tree.map(lambda kept, changed: jnp.where(first_row, kept, changed), recurrence, rescaled)
    row_value = new_state[1] * jnp.exp2(new_state[2])
    row_value = jnp.where(excess_degree < wave_limit, row_value, 0.0)
    return (new_state, row_value)

def legendre_table(wavenumbers, cumlog_part, cosine, sine_theta):
    wave_col = wavenumbers[:, None]
    log_start = -0.5 + 0.5 * cumlog_part[:, None] + wave_col * jnp.log2(sine_theta)[None, :]
    exponent = jnp.floor(log_start)
    leading = jnp.exp2(log_start - exponent)
    recurrence = (jnp.zeros_like(leading), leading, exponent)
    wave_limit = MMAX - wave_col

    def advance_one(carry, excess_degree):
        return advance(carry, excess_degree, wave_col, cosine[None, :], wave_limit)
    _, row_values = lax.scan(advance_one, recurrence, jnp.arange(MMAX, dtype=wavenumbers.dtype))
    return jnp.transpose(row_values, (1, 0, 2))

def implicit(vort_part, div_part, height_part, degree, geopot):
    lap_ratio = degree * (degree + 1.0) / (MMAX * MMAX)
    coupling = jnp.sqrt(lap_ratio)
    damping = 1.0 / (1.0 + diffusion * lap_ratio * lap_ratio)
    div_new = (div_part + coupling * height_part) / (1.0 + geopot * coupling * coupling)
    height_new = height_part - geopot * coupling * div_new
    return (damping * vort_part, damping * div_new, damping * height_new)

def reference(vorticity, divergence, height, mean_geopot):
    float_type = vorticity.dtype
    fields = jnp.stack([vorticity, divergence, height])
    spectrum = jnp.fft.rfft(fields, axis=-1)[..., :MMAX] / NLON
    coeffs = jnp.stack([jnp.real(spectrum), jnp.imag(spectrum)]).astype(float_type)
    row_index = jnp.arange(NLAT, dtype=float_type)
    cosine, sine_theta = latitudes(row_index)
    weight = jnp.pi * sine_theta / (NLAT + 0.5)
    wavenumbers = jnp.arange(MMAX, dtype=float_type)
    excess = jnp.maximum(wavenumbers[None, :] - MMAX * sine_theta[:, None] / cap_sine, 0.0) / filter_width
    coeffs = coeffs * (weight[:, None] * jnp.exp(-0.5 * excess * excess))
    cumlog = sector_logs(float_type)
    block_count = MMAX // 16
    wave_blocks = jnp.moveaxis(coeffs.reshape(2, 3, LEV, NLAT, block_count, 16), 4, 0)

    def solve_block(pair_args):
        block_index, wave_block = pair_args
        wave_index = block_index * 16 + jnp.arange(16, dtype=jnp.int32)
        block_waves = wave_index.astype(float_type)
        legendre = legendre_table(block_waves, cumlog[wave_index], cosine, sine_theta)
        spectral = jnp.einsum('mkj,cfljm->cflmk', legendre, wave_block, precision=lax.Precision.HIGHEST)
        degree = block_waves[:, None] + jnp.arange(MMAX, dtype=float_type)[None, :]
        geopot = mean_geopot[:, None, None]
        new_v, new_d, new_h = implicit(spectral[:, 0], spectral[:, 1], spectral[:, 2], degree, geopot)
        updated = jnp.stack([new_v, new_d, new_h], axis=1)
        return jnp.einsum('mkj,cflmk->cfljm', legendre, updated, precision=lax.Precision.HIGHEST)
    synthesis = lax.map(solve_block, (jnp.arange(block_count, dtype=jnp.int32), wave_blocks))
    synthesis = jnp.moveaxis(synthesis, 0, 4).reshape(2, 3, LEV, NLAT, MMAX)
    complex_coeffs = lax.complex(synthesis[0], synthesis[1]) * NLON
    complex_coeffs = jnp.pad(complex_coeffs, ((0, 0), (0, 0), (0, 0), (0, NLON // 2 + 1 - MMAX)))
    result = jnp.fft.irfft(complex_coeffs, n=NLON, axis=-1).astype(float_type)
    return (result[0], result[1], result[2])
```

```python
import jax
import jax.numpy as jnp
import ml_dtypes
import numpy as np
from jax import lax
from jax.experimental import pallas as pl
from jax.experimental.pallas import tpu as pltpu
from jax.sharding import PartitionSpec as P

NLON = 2560
NLAT = 1280
MMAX = 1280
F32 = jnp.float32
BF16 = jnp.bfloat16
STEPS = 64
CHUNKS = MMAX // STEPS
TILES = 5
LANES = 128

cap_sine = 0.5
filter_width = 64.0
diffusion = 4.0
renorm_big = 2.0**64
renorm_step = 64.0


def split_np(values):
    values = np.asarray(values, np.float64).astype(np.float32)
    high = values.astype(ml_dtypes.bfloat16)
    low = (values - high.astype(np.float32)).astype(ml_dtypes.bfloat16)
    return high, low


def latitude_rows():
    rows = np.arange(NLAT // 2, dtype=np.float64)
    colatitude = (4.0 * rows + 3.0) * np.pi / (4.0 * NLAT + 2.0)
    shortfall = 1.0 / (8.0 * NLAT * NLAT) - 1.0 / (8.0 * NLAT * NLAT * NLAT)
    one_minus = shortfall + 2.0 * (1.0 - shortfall) * np.sin(0.5 * colatitude) ** 2
    one_plus = shortfall + 2.0 * (1.0 - shortfall) * np.cos(0.5 * colatitude) ** 2
    cosine = 0.5 * (one_plus - one_minus)
    sine = np.sqrt(one_minus * one_plus)
    weight = np.pi * sine / (NLAT + 0.5)
    log_sine = np.log2(sine)
    log_high = np.round(log_sine * 256.0) / 256.0
    log_low = log_sine - log_high
    table = np.stack([cosine, log_high, log_low, MMAX * sine / cap_sine, weight])
    lane = np.arange(NLAT // 2)
    order = 10 * (lane % 64) + lane // 64
    full = np.zeros((8, NLAT // 2), np.float32)
    full[:5] = table[:, order]
    return full


def sector_logs():
    order = np.arange(1, MMAX, dtype=np.float64)
    terms = np.log2((2.0 * order + 1.0) / (2.0 * order))
    return (-0.5 + 0.5 * np.concatenate([[0.0], np.cumsum(terms)])).astype(np.float32)


def gather_matrix():
    out = np.zeros((10, 3, 2, 2, 2, 256), np.float32)
    for u in range(10):
        for f in range(3):
            for q in range(2):
                for c in range(2):
                    for lev in range(2):
                        out[u, f, q, c, lev, q * 128 + c * 64 + (2 * f + lev) * 10 + u] = 1.0
    return out.reshape(240, 256).astype(ml_dtypes.bfloat16)


def fold_matrix():
    out = np.zeros((4, 128, 2, 128), np.float32)
    for src in range(64):
        out[0, src, :, src] = 1.0
        out[1, src, :, 64 + src] = 1.0
        out[2, 127 - src, 0, src] = 1.0
        out[2, 127 - src, 1, src] = -1.0
        out[3, 127 - src, 0, 64 + src] = 1.0
        out[3, 127 - src, 1, 64 + src] = -1.0
    return out.reshape(512, 256).astype(ml_dtypes.bfloat16)


def unfold_matrix():
    out = np.zeros((4, 64, 2, 128), np.float32)
    for row in range(64):
        out[0, row, :, row] = 1.0
        out[1, row, :, 64 + row] = 1.0
        out[2, row, 0, 63 - row] = 1.0
        out[2, row, 1, 63 - row] = -1.0
        out[3, row, 0, 127 - row] = 1.0
        out[3, row, 1, 127 - row] = -1.0
    return out.reshape(256, 256).astype(ml_dtypes.bfloat16)


def scatter_matrix():
    out = np.zeros((2, 2, 5, 8, 128), np.float32)
    for c in range(2):
        for h in range(2):
            for i in range(5):
                for f in range(3):
                    for lev in range(2):
                        out[c, h, i, 2 * f + lev, 40 * f + 4 * (5 * h + i) + 2 * c + lev] = 1.0
    return out.reshape(160, 128).astype(ml_dtypes.bfloat16)


def forward_matrix():
    angle = 2.0 * np.pi * (np.outer(np.arange(64), np.arange(128)) % 128) / 128.0
    table = np.concatenate([np.cos(angle), np.sin(angle)], axis=1) / NLON
    high, low = split_np(table)
    return np.concatenate([high, low], axis=0)


def inverse_matrix():
    angle = 2.0 * np.pi * (np.outer(np.arange(64), np.arange(128)) % 128) / 128.0
    cosine = np.cos(angle).reshape(2, 1, 32, 128)
    sine = np.sin(angle).reshape(2, 1, 32, 128)
    real_part = np.concatenate([cosine, sine], axis=-1)
    imag_part = np.concatenate([-sine, cosine], axis=-1)
    table = np.broadcast_to(np.stack([real_part, imag_part]), (2, 2, 4, 32, 256)).reshape(512, 256)
    high, low = split_np(table)
    return np.concatenate([high, low], axis=0)


def twiddles():
    angle = 2.0 * np.pi * np.outer(np.arange(20), np.arange(128)) / NLON
    return np.stack([np.cos(angle), np.sin(angle)], axis=1).reshape(40, 128).astype(np.float32)


def split(values):
    high = values.astype(BF16)
    return high, (values - high.astype(F32)).astype(BF16)


def dot(left, right):
    return lax.dot_general(left, right, (((1,), (0,)), ((), ())), preferred_element_type=F32)


def dot_t(left, right):
    return lax.dot_general(left, right, (((1,), (1,)), ((), ())), preferred_element_type=F32)


C1, C2 = float(np.cos(2 * np.pi / 5)), float(np.cos(4 * np.pi / 5))
S1, S2 = float(np.sin(2 * np.pi / 5)), float(np.sin(4 * np.pi / 5))


def pack_kernel(vort_ref, div_ref, height_ref, out_ref):
    for b in range(4):
        for f, ref in enumerate((vort_ref, div_ref, height_ref)):
            for lev in range(2):
                out_ref[b, pl.ds((2 * f + lev) * 10, 10), :] = ref[lev, pl.ds(10 * b, 10), :]
        out_ref[b, pl.ds(60, 4), :] = jnp.zeros((4, 640), F32)


def unpack_kernel(in_ref, vort_ref, div_ref, height_ref):
    for b in range(4):
        for f, ref in enumerate((vort_ref, div_ref, height_ref)):
            for lev in range(2):
                ref[lev, pl.ds(10 * b, 10), :] = in_ref[b, pl.ds((2 * f + lev) * 10, 10), :]


def forward_kernel(in_ref, twiddle_ref, table_ref, out_ref, z_ref):
    @pl.loop(0, 8)
    def _(group):
        rows = pl.ds(pl.multiple_of(group * 8, 8), 8)
        x = [in_ref[i2 // 5, rows, pl.ds((i2 % 5) * 128, 128)] for i2 in range(20)]
        parts = []
        for n4 in range(4):
            v = [x[(4 * n5 + 5 * n4) % 20] for n5 in range(5)]
            p1, p2 = v[1] + v[4], v[2] + v[3]
            q1, q2 = v[1] - v[4], v[2] - v[3]
            parts.append(
                (
                    (v[0] + p1 + p2, None),
                    (v[0] + C1 * p1 + C2 * p2, -(S1 * q1 + S2 * q2)),
                    (v[0] + C2 * p1 + C1 * p2, S1 * q2 - S2 * q1),
                )
            )
        y = {}
        zero = jnp.zeros_like(x[0])
        g = [parts[n4][0][0] for n4 in range(4)]
        y[0, 0] = (g[0] + g[2] + (g[1] + g[3]), zero)
        y[2, 0] = (g[0] + g[2] - (g[1] + g[3]), zero)
        y[1, 0] = (g[0] - g[2], g[3] - g[1])
        y[3, 0] = (g[0] - g[2], g[1] - g[3])
        for b5 in (1, 2):
            re = [parts[n4][b5][0] for n4 in range(4)]
            im = [parts[n4][b5][1] for n4 in range(4)]
            er, ei = re[0] + re[2], im[0] + im[2]
            odr, odi = re[1] + re[3], im[1] + im[3]
            dr, di = re[0] - re[2], im[0] - im[2]
            fr, fi = re[1] - re[3], im[1] - im[3]
            y[0, b5] = (er + odr, ei + odi)
            y[2, b5] = (er - odr, ei - odi)
            y[1, b5] = (dr + fi, di - fr)
            y[3, b5] = (dr - fi, di + fr)
        for b in range(20):
            if b % 5 <= 2:
                yr, yi = y[b % 4, b % 5]
            else:
                yr, yi = y[-b % 4, 5 - b % 5]
                yi = -yi
            tr = twiddle_ref[pl.ds(2 * b, 1), :]
            ti = twiddle_ref[pl.ds(2 * b + 1, 1), :]
            z_ref[b, rows, pl.ds(0, 128)] = yr * tr + yi * ti
            z_ref[b, rows, pl.ds(128, 128)] = yi * tr - yr * ti

    table = table_ref[...]
    for b in range(20):
        re = z_ref[b, :, pl.ds(0, 128)]
        im = z_ref[b, :, pl.ds(128, 128)]
        re_hi, re_lo = split(re)
        im_hi, im_lo = split(im)

        def both(real, imag):
            top = jnp.concatenate([real, imag], axis=1)
            return jnp.concatenate([top, jnp.concatenate([imag, -real], axis=1)], axis=0)

        first = dot_t(table, both(re_hi, im_hi))
        total = first[:64] + first[64:] + dot_t(table[:64], both(re_lo, im_lo))
        for h in range(2):
            out_ref[pl.ds((b // 5) * 32, 32), pl.ds((5 * h + b % 5) * 128, 128)] = total[
                h * 32 : (h + 1) * 32
            ]


def inverse_kernel(in_ref, scatter_ref, twiddle_ref, table_ref, out_ref, c_ref, z_ref):
    for part in range(4):
        for i in range(5):
            c_ref[part, i, pl.ds(56, 8), :] = jnp.zeros((8, LANES), F32)
    for u in range(10):
        high, low = split(in_ref[:, pl.ds(u * 128, 128)])
        moved = dot_t(scatter_ref[...], high) + dot_t(scatter_ref[...], low)
        for part in range(4):
            for i in range(5):
                start = (part * 5 + i) * 8
                c_ref[part, i, pl.ds(u, 6, stride=10), :] = moved[start : start + 6]
    table_hi = table_ref[pl.ds(0, 512), :]
    table_lo = table_ref[pl.ds(512, 512), :]
    lane_owner = (lax.broadcasted_iota(jnp.int32, (64, 512), 1) % 128) // 32
    for i in range(5):
        block = jnp.concatenate([c_ref[part, i] for part in range(4)], axis=1)
        for b1 in range(4):
            high, low = split(jnp.where(lane_owner == b1, block, 0.0))
            first = dot(jnp.concatenate([high, low], axis=0), table_hi)
            z_ref[5 * b1 + i] = first[:64] + first[64:] + dot(high, table_lo)

    @pl.loop(0, 8)
    def _(group):
        rows = pl.ds(pl.multiple_of(group * 8, 8), 8)
        z = {}
        for b in range(20):
            zr = z_ref[b, rows, pl.ds(0, 128)]
            zi = z_ref[b, rows, pl.ds(128, 128)]
            tr = twiddle_ref[pl.ds(2 * b, 1), :]
            ti = twiddle_ref[pl.ds(2 * b + 1, 1), :]
            z[b % 4, b % 5] = (zr * tr - zi * ti, zr * ti + zi * tr)
        parts = [[None] * 5 for _ in range(4)]
        for b5 in range(5):
            r0, i0 = z[0, b5]
            r1, i1 = z[1, b5]
            r2, i2 = z[2, b5]
            r3, i3 = z[3, b5]
            er, ei, dr, di = r0 + r2, i0 + i2, r0 - r2, i0 - i2
            sr, si, fr, fi = r1 + r3, i1 + i3, r1 - r3, i1 - i3
            parts[0][b5] = (er + sr, ei + si)
            parts[2][b5] = (er - sr, ei - si)
            parts[1][b5] = (dr - fi, di + fr)
            parts[3][b5] = (dr + fi, di - fr)
        for n4 in range(4):
            t = parts[n4]
            base = t[0][0]
            p1, p2 = t[1][0] + t[4][0], t[2][0] + t[3][0]
            q1, q2 = t[1][1] - t[4][1], t[2][1] - t[3][1]
            m1, m2 = base + C1 * p1 + C2 * p2, base + C2 * p1 + C1 * p2
            n1, n2 = S1 * q1 + S2 * q2, S2 * q1 - S1 * q2
            for n5, value in enumerate((base + p1 + p2, m1 - n1, m2 - n2, m2 + n2, m1 + n1)):
                i2 = (4 * n5 + 5 * n4) % 20
                out_ref[i2 // 5, rows, pl.ds((i2 % 5) * 128, 128)] = value


def legendre_kernel(
    rank_ref,
    logs_ref,
    geo_ref,
    in_ref,
    lat_ref,
    gather_ref,
    fold_ref,
    unfold_ref,
    out_ref,
    a_ref,
    x_ref,
    coef_ref,
    state_ref,
    reset_ref,
    even_ref,
    odd_ref,
    acc_ref,
):
    rank = rank_ref[0]
    first = (rank % 32) * 20 + (rank // 32) * 5
    sub = lax.broadcasted_iota(jnp.int32, (8, LANES), 0)
    lane = lax.broadcasted_iota(jnp.int32, (8, LANES), 1)

    for u in range(10):
        a_ref[u, pl.ds(120, 8), :] = jnp.zeros((8, LANES), F32)
    for pair in range(5):
        high, low = split(in_ref[:, pl.ds(pair * 256, 256)])
        moved = dot_t(gather_ref[...], high) + dot_t(gather_ref[...], low)
        for u in range(10):
            for f in range(3):
                start = (u * 3 + f) * 8
                a_ref[u, pl.ds(f * 40 + pair * 8, 8), :] = moved[start : start + 8]

    for v in range(TILES):
        lanes = pl.ds(v * LANES, LANES)
        joined = jnp.concatenate(
            [a_ref[2 * v], a_ref[2 * v + 1], a_ref[9 - 2 * v], a_ref[8 - 2 * v]], axis=1
        )
        high, low = split(joined)
        folded = dot(high, fold_ref[...]) + dot(low, fold_ref[...])
        cut = lat_ref[pl.ds(3, 1), lanes]
        weight = lat_ref[pl.ds(4, 1), lanes]
        factors = []
        for pair in range(5):
            q = 2 * pair + sub // 4
            wave = first + q + jnp.where(q >= 5, 635, 0)
            excess = jnp.maximum(wave.astype(F32) - cut, 0.0) / filter_width
            doubling = jnp.where(wave == 0, 1.0, 2.0)
            factors.append(weight * jnp.exp(-0.5 * excess * excess) * doubling)
        factors = jnp.concatenate(factors * 3 + [jnp.zeros((8, LANES), F32)], axis=0)
        for parity in range(2):
            high, low = split(folded[:, parity * LANES : (parity + 1) * LANES] * factors)
            x_ref[parity, pl.ds(0, 128), lanes] = high
            x_ref[parity, pl.ds(128, 128), lanes] = low

    for phase in range(2):
        shift = jnp.where(sub >= 5, 635 + 3 * phase, 0)
        wave = (first + sub + shift).astype(F32)
        logs = jnp.zeros((8, LANES), F32)
        for slot in range(8):
            offset = slot + (635 + 3 * phase if slot >= 5 else 0)
            offset = min(offset, 644)
            logs = jnp.where(sub == slot, logs_ref[first + offset], logs)
        for v in range(TILES):
            lanes = pl.ds(v * LANES, LANES)
            main = wave * lat_ref[pl.ds(1, 1), lanes]
            rest = wave * lat_ref[pl.ds(2, 1), lanes] + logs
            exponent = jnp.floor(main + rest)
            reset_ref[phase, 0, :, lanes] = -jnp.exp2((main - exponent) + rest)
            reset_ref[phase, 1, :, lanes] = exponent

    def coefficients(block, _):
        step = block * STEPS + lane
        late = (sub >= 5) & (block >= CHUNKS // 2)
        wave_now = first + sub + jnp.where(sub >= 5, 635, 0) + jnp.where(late, 3, 0)
        excess = step - jnp.where(late, MMAX // 2, 0)
        live = (wave_now + excess < MMAX) & (jnp.logical_not(late) | (sub < 7))
        wave = wave_now.astype(F32)
        k = excess.astype(F32)
        degree = wave + k
        growth = jnp.sqrt((4.0 * degree * degree - 1.0) / jnp.maximum(k * (2.0 * wave + k), 1.0))
        backward = jnp.sqrt(
            jnp.maximum((k - 1.0) * (2.0 * wave + k - 1.0), 0.0)
            / jnp.maximum(4.0 * (degree - 1.0) * (degree - 1.0) - 1.0, 1.0)
        )
        start = excess == 0
        coef_ref[block, 0] = jnp.where(live & jnp.logical_not(start), growth, 0.0)
        coef_ref[block, 1] = jnp.where(live, jnp.where(start, 1.0, growth * backward), 0.0)
        return 0

    lax.fori_loop(0, CHUNKS + 1, coefficients, 0)
    for v in range(TILES):
        lanes = pl.ds(v * LANES, LANES)
        state_ref[0, :, lanes] = jnp.zeros((8, LANES), F32)
        state_ref[1, :, lanes] = reset_ref[0, 0, :, lanes]
        state_ref[2, :, lanes] = reset_ref[0, 1, :, lanes]
    acc_ref[...] = jnp.zeros_like(acc_ref)

    def generate(block, buf_ref):
        swap = (sub >= 5) & (block == CHUNKS // 2)
        newer, older, power, scale, cosine = [], [], [], [], []
        for v in range(TILES):
            lanes = pl.ds(v * LANES, LANES)
            newer.append(jnp.where(swap, 0.0, state_ref[0, :, lanes]))
            older.append(jnp.where(swap, reset_ref[1, 0, :, lanes], state_ref[1, :, lanes]))
            power.append(jnp.where(swap, reset_ref[1, 1, :, lanes], state_ref[2, :, lanes]))
            cosine.append(jnp.broadcast_to(lat_ref[pl.ds(0, 1), lanes], (8, LANES)))
            scale.append(jnp.where(power[v] < -126.0, 0.0, jnp.exp2(power[v])))
        growth = coef_ref[block, 0]
        backward = coef_ref[block, 1]
        held = {}
        for t in range(STEPS):
            a = jnp.broadcast_to(growth[:, t : t + 1], (8, LANES))
            c = jnp.broadcast_to(backward[:, t : t + 1], (8, LANES))
            for v in range(TILES):
                value = (a * cosine[v]) * newer[v] - c * older[v]
                older[v], newer[v] = newer[v], value
                held[t, v] = value * scale[v]
            if t % 8 == 7:
                for v in range(TILES):
                    large = jnp.abs(newer[v]) > renorm_big
                    factor = jnp.where(large, 1.0 / renorm_big, 1.0)
                    newer[v] = newer[v] * factor
                    older[v] = older[v] * factor
                    power[v] = power[v] + jnp.where(large, renorm_step, 0.0)
                    scale[v] = jnp.where(power[v] < -126.0, 0.0, jnp.exp2(power[v]))
            if t % 4 == 3:
                rows = pl.ds((t // 4) * 16, 16)
                for v in range(TILES):
                    lanes = pl.ds(v * LANES, LANES)
                    for parity in range(2):
                        both = jnp.concatenate(
                            [held.pop((t - 3 + parity, v)), held.pop((t - 1 + parity, v))], axis=0
                        )
                        high, low = split(both)
                        buf_ref[parity, 0, rows, lanes] = high
                        buf_ref[parity, 1, rows, lanes] = low
        for v in range(TILES):
            lanes = pl.ds(v * LANES, LANES)
            state_ref[0, :, lanes] = newer[v]
            state_ref[1, :, lanes] = older[v]
            state_ref[2, :, lanes] = power[v]

    geopot = jnp.where(sub % 2 == 0, geo_ref[0], geo_ref[1])

    def apply(block, buf_ref):
        late = block >= CHUNKS // 2
        slot = lane % 8
        upper = slot >= 5
        wave = first + slot + jnp.where(upper, jnp.where(late, 638 - MMAX // 2, 635), 0)
        owner = slot + jnp.where(upper & late, 3, 0)
        for parity in range(2):
            table_hi = buf_ref[parity, 0]
            table_lo = buf_ref[parity, 1]
            both = dot_t(x_ref[parity], table_hi)
            spectral = both[:128] + both[128:] + dot_t(x_ref[parity, pl.ds(0, 128), :], table_lo)
            halves = []
            for half in range(2):
                step = block * STEPS + 2 * (half * 16 + lane // 8) + parity
                degree = (wave + step).astype(F32)
                ratio = degree * (degree + 1.0) * (1.0 / (MMAX * MMAX))
                coupling = jnp.sqrt(ratio)
                damping = 1.0 / (1.0 + diffusion * ratio * ratio)
                shared = damping / (1.0 + geopot * ratio)
                cross = geopot * coupling
                vort, div, height = [], [], []
                for pair in range(5):
                    mine = owner == 2 * pair + sub // 4
                    part = spectral[:, half * LANES : (half + 1) * LANES]
                    v_part = part[pair * 8 : pair * 8 + 8]
                    d_part = part[40 + pair * 8 : 48 + pair * 8]
                    h_part = part[80 + pair * 8 : 88 + pair * 8]
                    mixed = jnp.where(mine, shared, 0.0)
                    vort.append(jnp.where(mine, damping, 0.0) * v_part)
                    div.append(mixed * (d_part + coupling * h_part))
                    height.append(mixed * (h_part - cross * d_part))
                halves.append(
                    jnp.concatenate(vort + div + height + [jnp.zeros((8, LANES), F32)], axis=0)
                )
            high, low = split(jnp.concatenate(halves, axis=1))
            both = dot(jnp.concatenate([high, low], axis=0), table_hi)
            acc_ref[parity] += both[:128] + both[128:] + dot(high, table_lo)

    generate(0, even_ref)

    @pl.loop(0, CHUNKS // 2)
    def _(pair):
        generate(2 * pair + 1, odd_ref)
        apply(2 * pair, even_ref)
        generate(2 * pair + 2, even_ref)
        apply(2 * pair + 1, odd_ref)

    for v in range(TILES):
        lanes = pl.ds(v * LANES, LANES)
        joined = jnp.concatenate([acc_ref[0, :, lanes], acc_ref[1, :, lanes]], axis=1)
        high, low = split(joined)
        moved = dot_t(unfold_ref[...], high) + dot_t(unfold_ref[...], low)
        for part, u in enumerate((2 * v, 2 * v + 1, 9 - 2 * v, 8 - 2 * v)):
            out_ref[pl.ds((part // 2) * 64, 64), pl.ds(u * LANES, LANES)] = moved[
                part * 64 : part * 64 + 64
            ]


VMEM = pl.BlockSpec(memory_space=pltpu.VMEM)
SMEM = pl.BlockSpec(memory_space=pltpu.SMEM)


def call(kernel, outputs, specs, scratch, megabytes, flops, name):
    shapes = tuple(jax.ShapeDtypeStruct(shape, F32) for shape in outputs)
    single = len(shapes) == 1
    return pl.pallas_call(
        kernel,
        out_shape=shapes[0] if single else shapes,
        in_specs=specs,
        out_specs=VMEM if single else tuple(VMEM for _ in shapes),
        scratch_shapes=scratch,
        compiler_params=pltpu.CompilerParams(vmem_limit_bytes=megabytes << 20),
        cost_estimate=pl.CostEstimate(flops=flops, bytes_accessed=2 << 20, transcendentals=0),
        name=name,
    )


def shards(vorticity, divergence, height, mean_geopot):
    rank = lax.axis_index("lat") * lax.axis_size("lon") + lax.axis_index("lon")
    rank = rank.astype(jnp.int32).reshape(1)
    twiddle = jnp.asarray(twiddles())
    packed = call(pack_kernel, [(4, 64, 640)], [VMEM] * 3, [], 8, 1 << 20, "pack")(
        vorticity, divergence, height
    )
    sectors = lax.all_to_all(packed, "lon", split_axis=0, concat_axis=0, tiled=True)
    spectrum = call(
        forward_kernel,
        [(128, 1280)],
        [VMEM] * 3,
        [pltpu.VMEM((20, 64, 256), F32)],
        16,
        1 << 28,
        "forward",
    )(sectors, twiddle, jnp.asarray(forward_matrix()))
    columns = lax.all_to_all(spectrum, ("lat", "lon"), split_axis=0, concat_axis=0, tiled=True)
    synthesis = call(
        legendre_kernel,
        [(128, 1280)],
        [SMEM] * 3 + [VMEM] * 5,
        [
            pltpu.VMEM((10, 128, LANES), F32),
            pltpu.VMEM((2, 256, 640), BF16),
            pltpu.VMEM((CHUNKS + 1, 2, 8, LANES), F32),
            pltpu.VMEM((3, 8, 640), F32),
            pltpu.VMEM((2, 2, 8, 640), F32),
            pltpu.VMEM((2, 2, 256, 640), BF16),
            pltpu.VMEM((2, 2, 256, 640), BF16),
            pltpu.VMEM((2, 128, 640), F32),
        ],
        32,
        1 << 33,
        "legendre",
    )(
        rank,
        jnp.asarray(sector_logs()),
        mean_geopot,
        columns,
        jnp.asarray(latitude_rows()),
        jnp.asarray(gather_matrix()),
        jnp.asarray(fold_matrix()),
        jnp.asarray(unfold_matrix()),
    )
    gathered = lax.all_to_all(synthesis, ("lat", "lon"), split_axis=0, concat_axis=0, tiled=True)
    result = call(
        inverse_kernel,
        [(4, 64, 640)],
        [VMEM] * 4,
        [pltpu.VMEM((4, 5, 64, LANES), F32), pltpu.VMEM((20, 64, 256), F32)],
        16,
        1 << 28,
        "inverse",
    )(gathered, jnp.asarray(scatter_matrix()), twiddle, jnp.asarray(inverse_matrix()))
    pieces = lax.all_to_all(result, "lon", split_axis=0, concat_axis=0, tiled=True)
    return call(unpack_kernel, [(2, 40, 640)] * 3, [VMEM], [], 8, 1 << 20, "unpack")(pieces)


def solution(mesh):
    placed = (P(None, "lat", "lon"), P(None, "lat", "lon"), P(None, "lat", "lon"), P())
    return jax.shard_map(
        shards,
        mesh=mesh,
        in_specs=placed,
        out_specs=(P(None, "lat", "lon"), P(None, "lat", "lon"), P(None, "lat", "lon")),
        check_vma=False,
    )
```

```python
import jax
import jax.numpy as jnp
import ml_dtypes
import numpy as np
from jax import lax
from jax.experimental import pallas as pl
from jax.experimental.pallas import tpu as pltpu
from jax.sharding import PartitionSpec as P

NLON = 2560
NLAT = 1280
MMAX = 1280
F32 = jnp.float32
BF16 = jnp.bfloat16
STEPS = 64
CHUNKS = MMAX // STEPS
TILES = 5
LANES = 128

cap_sine = 0.5
filter_width = 64.0
diffusion = 4.0
renorm_big = 2.0**64
renorm_step = 64.0


def split_np(values):
    values = np.asarray(values, np.float64).astype(np.float32)
    high = values.astype(ml_dtypes.bfloat16)
    low = (values - high.astype(np.float32)).astype(ml_dtypes.bfloat16)
    return high, low


def latitude_rows():
    rows = np.arange(NLAT // 2, dtype=np.float64)
    colatitude = (4.0 * rows + 3.0) * np.pi / (4.0 * NLAT + 2.0)
    shortfall = 1.0 / (8.0 * NLAT * NLAT) - 1.0 / (8.0 * NLAT * NLAT * NLAT)
    one_minus = shortfall + 2.0 * (1.0 - shortfall) * np.sin(0.5 * colatitude) ** 2
    one_plus = shortfall + 2.0 * (1.0 - shortfall) * np.cos(0.5 * colatitude) ** 2
    cosine = 0.5 * (one_plus - one_minus)
    sine = np.sqrt(one_minus * one_plus)
    weight = np.pi * sine / (NLAT + 0.5)
    log_sine = np.log2(sine)
    log_high = np.round(log_sine * 256.0) / 256.0
    log_low = log_sine - log_high
    table = np.stack([cosine, log_high, log_low, MMAX * sine / cap_sine, weight])
    lane = np.arange(NLAT // 2)
    order = 10 * (lane % 64) + lane // 64
    full = np.zeros((8, NLAT // 2), np.float32)
    full[:5] = table[:, order]
    return full


def sector_logs():
    order = np.arange(1, MMAX, dtype=np.float64)
    terms = np.log2((2.0 * order + 1.0) / (2.0 * order))
    return (-0.5 + 0.5 * np.concatenate([[0.0], np.cumsum(terms)])).astype(np.float32)


def gather_matrix():
    out = np.zeros((10, 3, 2, 2, 2, 256), np.float32)
    for u in range(10):
        for f in range(3):
            for q in range(2):
                for c in range(2):
                    for lev in range(2):
                        out[u, f, q, c, lev, q * 128 + c * 64 + (2 * f + lev) * 10 + u] = 1.0
    return out.reshape(240, 256).astype(ml_dtypes.bfloat16)


def fold_matrix():
    out = np.zeros((4, 128, 2, 128), np.float32)
    for src in range(64):
        out[0, src, :, src] = 1.0
        out[1, src, :, 64 + src] = 1.0
        out[2, 127 - src, 0, src] = 1.0
        out[2, 127 - src, 1, src] = -1.0
        out[3, 127 - src, 0, 64 + src] = 1.0
        out[3, 127 - src, 1, 64 + src] = -1.0
    return out.reshape(512, 256).astype(ml_dtypes.bfloat16)


def unfold_matrix():
    out = np.zeros((4, 64, 2, 128), np.float32)
    for row in range(64):
        out[0, row, :, row] = 1.0
        out[1, row, :, 64 + row] = 1.0
        out[2, row, 0, 63 - row] = 1.0
        out[2, row, 1, 63 - row] = -1.0
        out[3, row, 0, 127 - row] = 1.0
        out[3, row, 1, 127 - row] = -1.0
    return out.reshape(256, 256).astype(ml_dtypes.bfloat16)


def scatter_matrix():
    out = np.zeros((2, 2, 5, 8, 128), np.float32)
    for c in range(2):
        for h in range(2):
            for i in range(5):
                for f in range(3):
                    for lev in range(2):
                        out[c, h, i, 2 * f + lev, 40 * f + 4 * (5 * h + i) + 2 * c + lev] = 1.0
    return out.reshape(160, 128).astype(ml_dtypes.bfloat16)


def forward_matrix():
    angle = 2.0 * np.pi * (np.outer(np.arange(64), np.arange(128)) % 128) / 128.0
    table = np.concatenate([np.cos(angle), np.sin(angle)], axis=1) / NLON
    high, low = split_np(table)
    return np.concatenate([high, low], axis=0)


def inverse_matrix():
    angle = 2.0 * np.pi * (np.outer(np.arange(64), np.arange(128)) % 128) / 128.0
    cosine = np.cos(angle).reshape(2, 1, 32, 128)
    sine = np.sin(angle).reshape(2, 1, 32, 128)
    real_part = np.concatenate([cosine, sine], axis=-1)
    imag_part = np.concatenate([-sine, cosine], axis=-1)
    table = np.broadcast_to(np.stack([real_part, imag_part]), (2, 2, 4, 32, 256)).reshape(512, 256)
    high, low = split_np(table)
    return np.concatenate([high, low], axis=0)


def twiddles():
    angle = 2.0 * np.pi * np.outer(np.arange(20), np.arange(128)) / NLON
    return np.stack([np.cos(angle), np.sin(angle)], axis=1).reshape(40, 128).astype(np.float32)


def split(values):
    high = values.astype(BF16)
    return high, (values - high.astype(F32)).astype(BF16)


def dot(left, right):
    return lax.dot_general(left, right, (((1,), (0,)), ((), ())), preferred_element_type=F32)


def dot_t(left, right):
    return lax.dot_general(left, right, (((1,), (1,)), ((), ())), preferred_element_type=F32)


C1, C2 = float(np.cos(2 * np.pi / 5)), float(np.cos(4 * np.pi / 5))
S1, S2 = float(np.sin(2 * np.pi / 5)), float(np.sin(4 * np.pi / 5))


def pack_kernel(vort_ref, div_ref, height_ref, out_ref):
    for b in range(4):
        for f, ref in enumerate((vort_ref, div_ref, height_ref)):
            for lev in range(2):
                out_ref[b, pl.ds((2 * f + lev) * 10, 10), :] = ref[lev, pl.ds(10 * b, 10), :]
        out_ref[b, pl.ds(60, 4), :] = jnp.zeros((4, 640), F32)


def unpack_kernel(in_ref, vort_ref, div_ref, height_ref):
    for b in range(4):
        for f, ref in enumerate((vort_ref, div_ref, height_ref)):
            for lev in range(2):
                ref[lev, pl.ds(10 * b, 10), :] = in_ref[b, pl.ds((2 * f + lev) * 10, 10), :]


def forward_kernel(in_ref, twiddle_ref, table_ref, out_ref, z_ref):
    @pl.loop(0, 8)
    def _(group):
        rows = pl.ds(pl.multiple_of(group * 8, 8), 8)
        x = [in_ref[i2 // 5, rows, pl.ds((i2 % 5) * 128, 128)] for i2 in range(20)]
        parts = []
        for n4 in range(4):
            v = [x[(4 * n5 + 5 * n4) % 20] for n5 in range(5)]
            p1, p2 = v[1] + v[4], v[2] + v[3]
            q1, q2 = v[1] - v[4], v[2] - v[3]
            parts.append(
                (
                    (v[0] + p1 + p2, None),
                    (v[0] + C1 * p1 + C2 * p2, -(S1 * q1 + S2 * q2)),
                    (v[0] + C2 * p1 + C1 * p2, S1 * q2 - S2 * q1),
                )
            )
        y = {}
        zero = jnp.zeros_like(x[0])
        g = [parts[n4][0][0] for n4 in range(4)]
        y[0, 0] = (g[0] + g[2] + (g[1] + g[3]), zero)
        y[2, 0] = (g[0] + g[2] - (g[1] + g[3]), zero)
        y[1, 0] = (g[0] - g[2], g[3] - g[1])
        y[3, 0] = (g[0] - g[2], g[1] - g[3])
        for b5 in (1, 2):
            re = [parts[n4][b5][0] for n4 in range(4)]
            im = [parts[n4][b5][1] for n4 in range(4)]
            er, ei = re[0] + re[2], im[0] + im[2]
            odr, odi = re[1] + re[3], im[1] + im[3]
            dr, di = re[0] - re[2], im[0] - im[2]
            fr, fi = re[1] - re[3], im[1] - im[3]
            y[0, b5] = (er + odr, ei + odi)
            y[2, b5] = (er - odr, ei - odi)
            y[1, b5] = (dr + fi, di - fr)
            y[3, b5] = (dr - fi, di + fr)
        for b in range(20):
            if b % 5 <= 2:
                yr, yi = y[b % 4, b % 5]
            else:
                yr, yi = y[-b % 4, 5 - b % 5]
                yi = -yi
            tr = twiddle_ref[pl.ds(2 * b, 1), :]
            ti = twiddle_ref[pl.ds(2 * b + 1, 1), :]
            z_ref[b, rows, pl.ds(0, 128)] = yr * tr + yi * ti
            z_ref[b, rows, pl.ds(128, 128)] = yi * tr - yr * ti

    table = table_ref[...]
    for b in range(20):
        re = z_ref[b, :, pl.ds(0, 128)]
        im = z_ref[b, :, pl.ds(128, 128)]
        re_hi, re_lo = split(re)
        im_hi, im_lo = split(im)

        def both(real, imag):
            top = jnp.concatenate([real, imag], axis=1)
            return jnp.concatenate([top, jnp.concatenate([imag, -real], axis=1)], axis=0)

        first = dot_t(table, both(re_hi, im_hi))
        total = first[:64] + first[64:] + dot_t(table[:64], both(re_lo, im_lo))
        for h in range(2):
            out_ref[pl.ds((b // 5) * 32, 32), pl.ds((5 * h + b % 5) * 128, 128)] = total[
                h * 32 : (h + 1) * 32
            ]


def inverse_kernel(in_ref, scatter_ref, twiddle_ref, table_ref, out_ref, c_ref, z_ref):
    for part in range(4):
        for i in range(5):
            c_ref[part, i, pl.ds(56, 8), :] = jnp.zeros((8, LANES), F32)
    for u in range(10):
        high, low = split(in_ref[:, pl.ds(u * 128, 128)])
        moved = dot_t(scatter_ref[...], high) + dot_t(scatter_ref[...], low)
        for part in range(4):
            for i in range(5):
                start = (part * 5 + i) * 8
                c_ref[part, i, pl.ds(u, 6, stride=10), :] = moved[start : start + 6]
    table_hi = table_ref[pl.ds(0, 512), :]
    table_lo = table_ref[pl.ds(512, 512), :]
    lane_owner = (lax.broadcasted_iota(jnp.int32, (64, 512), 1) % 128) // 32
    for i in range(5):
        block = jnp.concatenate([c_ref[part, i] for part in range(4)], axis=1)
        for b1 in range(4):
            high, low = split(jnp.where(lane_owner == b1, block, 0.0))
            first = dot(jnp.concatenate([high, low], axis=0), table_hi)
            z_ref[5 * b1 + i] = first[:64] + first[64:] + dot(high, table_lo)

    @pl.loop(0, 8)
    def _(group):
        rows = pl.ds(pl.multiple_of(group * 8, 8), 8)
        z = {}
        for b in range(20):
            zr = z_ref[b, rows, pl.ds(0, 128)]
            zi = z_ref[b, rows, pl.ds(128, 128)]
            tr = twiddle_ref[pl.ds(2 * b, 1), :]
            ti = twiddle_ref[pl.ds(2 * b + 1, 1), :]
            z[b % 4, b % 5] = (zr * tr - zi * ti, zr * ti + zi * tr)
        parts = [[None] * 5 for _ in range(4)]
        for b5 in range(5):
            r0, i0 = z[0, b5]
            r1, i1 = z[1, b5]
            r2, i2 = z[2, b5]
            r3, i3 = z[3, b5]
            er, ei, dr, di = r0 + r2, i0 + i2, r0 - r2, i0 - i2
            sr, si, fr, fi = r1 + r3, i1 + i3, r1 - r3, i1 - i3
            parts[0][b5] = (er + sr, ei + si)
            parts[2][b5] = (er - sr, ei - si)
            parts[1][b5] = (dr - fi, di + fr)
            parts[3][b5] = (dr + fi, di - fr)
        for n4 in range(4):
            t = parts[n4]
            base = t[0][0]
            p1, p2 = t[1][0] + t[4][0], t[2][0] + t[3][0]
            q1, q2 = t[1][1] - t[4][1], t[2][1] - t[3][1]
            m1, m2 = base + C1 * p1 + C2 * p2, base + C2 * p1 + C1 * p2
            n1, n2 = S1 * q1 + S2 * q2, S2 * q1 - S1 * q2
            for n5, value in enumerate((base + p1 + p2, m1 - n1, m2 - n2, m2 + n2, m1 + n1)):
                i2 = (4 * n5 + 5 * n4) % 20
                out_ref[i2 // 5, rows, pl.ds((i2 % 5) * 128, 128)] = value


def legendre_kernel(
    rank_ref,
    logs_ref,
    geo_ref,
    in_ref,
    lat_ref,
    gather_ref,
    fold_ref,
    unfold_ref,
    out_ref,
    a_ref,
    x_ref,
    coef_ref,
    state_ref,
    reset_ref,
    table0_ref,
    table1_ref,
    table2_ref,
    update0_ref,
    update1_ref,
    update2_ref,
    acc_ref,
):
    rank = rank_ref[0]
    first = (rank % 32) * 20 + (rank // 32) * 5
    sub = lax.broadcasted_iota(jnp.int32, (8, LANES), 0)
    lane = lax.broadcasted_iota(jnp.int32, (8, LANES), 1)

    for u in range(10):
        a_ref[u, pl.ds(120, 8), :] = jnp.zeros((8, LANES), F32)
    for pair in range(5):
        high, low = split(in_ref[:, pl.ds(pair * 256, 256)])
        moved = dot_t(gather_ref[...], high) + dot_t(gather_ref[...], low)
        for u in range(10):
            for f in range(3):
                start = (u * 3 + f) * 8
                a_ref[u, pl.ds(f * 40 + pair * 8, 8), :] = moved[start : start + 8]

    for v in range(TILES):
        lanes = pl.ds(v * LANES, LANES)
        joined = jnp.concatenate(
            [a_ref[2 * v], a_ref[2 * v + 1], a_ref[9 - 2 * v], a_ref[8 - 2 * v]], axis=1
        )
        high, low = split(joined)
        folded = dot(high, fold_ref[...]) + dot(low, fold_ref[...])
        cut = lat_ref[pl.ds(3, 1), lanes]
        weight = lat_ref[pl.ds(4, 1), lanes]
        factors = []
        for pair in range(5):
            q = 2 * pair + sub // 4
            wave = first + q + jnp.where(q >= 5, 635, 0)
            excess = jnp.maximum(wave.astype(F32) - cut, 0.0) / filter_width
            doubling = jnp.where(wave == 0, 1.0, 2.0)
            factors.append(weight * jnp.exp(-0.5 * excess * excess) * doubling)
        factors = jnp.concatenate(factors * 3 + [jnp.zeros((8, LANES), F32)], axis=0)
        for parity in range(2):
            high, low = split(folded[:, parity * LANES : (parity + 1) * LANES] * factors)
            x_ref[parity, pl.ds(0, 128), lanes] = high
            x_ref[parity, pl.ds(128, 128), lanes] = low

    for phase in range(2):
        shift = jnp.where(sub >= 5, 635 + 3 * phase, 0)
        wave = (first + sub + shift).astype(F32)
        logs = jnp.zeros((8, LANES), F32)
        for slot in range(8):
            offset = slot + (635 + 3 * phase if slot >= 5 else 0)
            offset = min(offset, 644)
            logs = jnp.where(sub == slot, logs_ref[first + offset], logs)
        for v in range(TILES):
            lanes = pl.ds(v * LANES, LANES)
            main = wave * lat_ref[pl.ds(1, 1), lanes]
            rest = wave * lat_ref[pl.ds(2, 1), lanes] + logs
            exponent = jnp.floor(main + rest)
            reset_ref[phase, 0, :, lanes] = -jnp.exp2((main - exponent) + rest)
            reset_ref[phase, 1, :, lanes] = exponent

    def coefficients(block, _):
        step = block * STEPS + lane
        late = (sub >= 5) & (block >= CHUNKS // 2)
        wave_now = first + sub + jnp.where(sub >= 5, 635, 0) + jnp.where(late, 3, 0)
        excess = step - jnp.where(late, MMAX // 2, 0)
        live = (wave_now + excess < MMAX) & (jnp.logical_not(late) | (sub < 7))
        wave = wave_now.astype(F32)
        k = excess.astype(F32)
        degree = wave + k
        growth = jnp.sqrt((4.0 * degree * degree - 1.0) / jnp.maximum(k * (2.0 * wave + k), 1.0))
        backward = jnp.sqrt(
            jnp.maximum((k - 1.0) * (2.0 * wave + k - 1.0), 0.0)
            / jnp.maximum(4.0 * (degree - 1.0) * (degree - 1.0) - 1.0, 1.0)
        )
        start = excess == 0
        coef_ref[block, 0] = jnp.where(live & jnp.logical_not(start), growth, 0.0)
        coef_ref[block, 1] = jnp.where(live, jnp.where(start, 1.0, growth * backward), 0.0)
        return 0

    lax.fori_loop(0, CHUNKS + 3, coefficients, 0)
    for v in range(TILES):
        lanes = pl.ds(v * LANES, LANES)
        state_ref[0, :, lanes] = jnp.zeros((8, LANES), F32)
        state_ref[1, :, lanes] = reset_ref[0, 0, :, lanes]
        state_ref[2, :, lanes] = reset_ref[0, 1, :, lanes]
    acc_ref[...] = jnp.zeros_like(acc_ref)

    def generate(block, buf_ref):
        swap = (sub >= 5) & (block == CHUNKS // 2)
        newer, older, power, scale, cosine = [], [], [], [], []
        for v in range(TILES):
            lanes = pl.ds(v * LANES, LANES)
            newer.append(jnp.where(swap, 0.0, state_ref[0, :, lanes]))
            older.append(jnp.where(swap, reset_ref[1, 0, :, lanes], state_ref[1, :, lanes]))
            power.append(jnp.where(swap, reset_ref[1, 1, :, lanes], state_ref[2, :, lanes]))
            cosine.append(jnp.broadcast_to(lat_ref[pl.ds(0, 1), lanes], (8, LANES)))
            scale.append(jnp.where(power[v] < -126.0, 0.0, jnp.exp2(power[v])))
        growth = coef_ref[block, 0]
        backward = coef_ref[block, 1]
        held = {}
        for t in range(STEPS):
            a = jnp.broadcast_to(growth[:, t : t + 1], (8, LANES))
            c = jnp.broadcast_to(backward[:, t : t + 1], (8, LANES))
            for v in range(TILES):
                value = (a * cosine[v]) * newer[v] - c * older[v]
                older[v], newer[v] = newer[v], value
                held[t, v] = value * scale[v]
            if t % 8 == 7:
                for v in range(TILES):
                    large = jnp.abs(newer[v]) > renorm_big
                    factor = jnp.where(large, 1.0 / renorm_big, 1.0)
                    newer[v] = newer[v] * factor
                    older[v] = older[v] * factor
                    power[v] = power[v] + jnp.where(large, renorm_step, 0.0)
                    scale[v] = jnp.where(power[v] < -126.0, 0.0, jnp.exp2(power[v]))
            if t % 4 == 3:
                rows = pl.ds((t // 4) * 16, 16)
                for v in range(TILES):
                    lanes = pl.ds(v * LANES, LANES)
                    for parity in range(2):
                        both = jnp.concatenate(
                            [held.pop((t - 3 + parity, v)), held.pop((t - 1 + parity, v))], axis=0
                        )
                        high, low = split(both)
                        buf_ref[parity, 0, rows, lanes] = high
                        buf_ref[parity, 1, rows, lanes] = low
        for v in range(TILES):
            lanes = pl.ds(v * LANES, LANES)
            state_ref[0, :, lanes] = newer[v]
            state_ref[1, :, lanes] = older[v]
            state_ref[2, :, lanes] = power[v]

    geopot = jnp.where(sub % 2 == 0, geo_ref[0], geo_ref[1])

    def analyse(block, parity, buf_ref, update_ref):
        late = block >= CHUNKS // 2
        slot = lane % 8
        upper = slot >= 5
        wave = first + slot + jnp.where(upper, jnp.where(late, 638 - MMAX // 2, 635), 0)
        owner = slot + jnp.where(upper & late, 3, 0)
        both = dot_t(x_ref[parity], buf_ref[parity, 0])
        spectral = both[:128] + both[128:] + dot_t(
            x_ref[parity, pl.ds(0, 128), :], buf_ref[parity, 1]
        )
        halves = []
        for half in range(2):
            step = block * STEPS + 2 * (half * 16 + lane // 8) + parity
            degree = (wave + step).astype(F32)
            ratio = degree * (degree + 1.0) * (1.0 / (MMAX * MMAX))
            coupling = jnp.sqrt(ratio)
            damping = 1.0 / (1.0 + diffusion * ratio * ratio)
            shared = damping / (1.0 + geopot * ratio)
            cross = geopot * coupling
            part = spectral[:, half * LANES : (half + 1) * LANES]
            vort, div, height = [], [], []
            for pair in range(5):
                mine = owner == 2 * pair + sub // 4
                v_part = part[pair * 8 : pair * 8 + 8]
                d_part = part[40 + pair * 8 : 48 + pair * 8]
                h_part = part[80 + pair * 8 : 88 + pair * 8]
                mixed = jnp.where(mine, shared, 0.0)
                vort.append(jnp.where(mine, damping, 0.0) * v_part)
                div.append(mixed * (d_part + coupling * h_part))
                height.append(mixed * (h_part - cross * d_part))
            halves.append(
                jnp.concatenate(vort + div + height + [jnp.zeros((8, LANES), F32)], axis=0)
            )
        high, low = split(jnp.concatenate(halves, axis=1))
        update_ref[parity, pl.ds(0, 128), :] = high
        update_ref[parity, pl.ds(128, 128), :] = low

    def synthesise(parity, buf_ref, update_ref):
        both = dot(update_ref[parity], buf_ref[parity, 0])
        rest = dot(update_ref[parity, pl.ds(0, 128), :], buf_ref[parity, 1])
        acc_ref[parity] += both[:128] + both[128:] + rest

    tables = (table0_ref, table1_ref, table2_ref)
    updates = (update0_ref, update1_ref, update2_ref)
    generate(0, tables[0])
    generate(1, tables[1])
    for parity in range(2):
        analyse(0, parity, tables[0], updates[0])

    @pl.loop(0, (CHUNKS + 2) // 3)
    def _(group):
        for turn in range(3):
            block = 3 * group + turn

            def advance(block=block, turn=turn):
                now, later, last = turn, (turn + 1) % 3, (turn + 2) % 3
                generate(block + 2, tables[last])
                for parity in range(2):
                    analyse(block + 1, parity, tables[later], updates[later])
                    synthesise(parity, tables[now], updates[now])

            if turn < 2:
                advance()
            else:
                pl.when(block < CHUNKS)(advance)

    for v in range(TILES):
        lanes = pl.ds(v * LANES, LANES)
        joined = jnp.concatenate([acc_ref[0, :, lanes], acc_ref[1, :, lanes]], axis=1)
        high, low = split(joined)
        moved = dot_t(unfold_ref[...], high) + dot_t(unfold_ref[...], low)
        for part, u in enumerate((2 * v, 2 * v + 1, 9 - 2 * v, 8 - 2 * v)):
            out_ref[pl.ds((part // 2) * 64, 64), pl.ds(u * LANES, LANES)] = moved[
                part * 64 : part * 64 + 64
            ]


VMEM = pl.BlockSpec(memory_space=pltpu.VMEM)
SMEM = pl.BlockSpec(memory_space=pltpu.SMEM)


def call(kernel, outputs, specs, scratch, megabytes, flops, name):
    shapes = tuple(jax.ShapeDtypeStruct(shape, F32) for shape in outputs)
    single = len(shapes) == 1
    return pl.pallas_call(
        kernel,
        out_shape=shapes[0] if single else shapes,
        in_specs=specs,
        out_specs=VMEM if single else tuple(VMEM for _ in shapes),
        scratch_shapes=scratch,
        compiler_params=pltpu.CompilerParams(vmem_limit_bytes=megabytes << 20),
        cost_estimate=pl.CostEstimate(flops=flops, bytes_accessed=2 << 20, transcendentals=0),
        name=name,
    )


def shards(vorticity, divergence, height, mean_geopot):
    rank = lax.axis_index("lat") * lax.axis_size("lon") + lax.axis_index("lon")
    rank = rank.astype(jnp.int32).reshape(1)
    twiddle = jnp.asarray(twiddles())
    packed = call(pack_kernel, [(4, 64, 640)], [VMEM] * 3, [], 8, 1 << 20, "pack")(
        vorticity, divergence, height
    )
    sectors = lax.all_to_all(packed, "lon", split_axis=0, concat_axis=0, tiled=True)
    spectrum = call(
        forward_kernel,
        [(128, 1280)],
        [VMEM] * 3,
        [pltpu.VMEM((20, 64, 256), F32)],
        16,
        1 << 28,
        "forward",
    )(sectors, twiddle, jnp.asarray(forward_matrix()))
    columns = lax.all_to_all(spectrum, ("lat", "lon"), split_axis=0, concat_axis=0, tiled=True)
    synthesis = call(
        legendre_kernel,
        [(128, 1280)],
        [SMEM] * 3 + [VMEM] * 5,
        [
            pltpu.VMEM((10, 128, LANES), F32),
            pltpu.VMEM((2, 256, 640), BF16),
            pltpu.VMEM((CHUNKS + 3, 2, 8, LANES), F32),
            pltpu.VMEM((3, 8, 640), F32),
            pltpu.VMEM((2, 2, 8, 640), F32),
            *[pltpu.VMEM((2, 2, 256, 640), BF16) for _ in range(3)],
            *[pltpu.VMEM((2, 256, 256), BF16) for _ in range(3)],
            pltpu.VMEM((2, 128, 640), F32),
        ],
        32,
        1 << 33,
        "legendre",
    )(
        rank,
        jnp.asarray(sector_logs()),
        mean_geopot,
        columns,
        jnp.asarray(latitude_rows()),
        jnp.asarray(gather_matrix()),
        jnp.asarray(fold_matrix()),
        jnp.asarray(unfold_matrix()),
    )
    gathered = lax.all_to_all(synthesis, ("lat", "lon"), split_axis=0, concat_axis=0, tiled=True)
    result = call(
        inverse_kernel,
        [(4, 64, 640)],
        [VMEM] * 4,
        [pltpu.VMEM((4, 5, 64, LANES), F32), pltpu.VMEM((20, 64, 256), F32)],
        16,
        1 << 28,
        "inverse",
    )(gathered, jnp.asarray(scatter_matrix()), twiddle, jnp.asarray(inverse_matrix()))
    pieces = lax.all_to_all(result, "lon", split_axis=0, concat_axis=0, tiled=True)
    return call(unpack_kernel, [(2, 40, 640)] * 3, [VMEM], [], 8, 1 << 20, "unpack")(pieces)


def solution(mesh):
    placed = (P(None, "lat", "lon"), P(None, "lat", "lon"), P(None, "lat", "lon"), P())
    return jax.shard_map(
        shards,
        mesh=mesh,
        in_specs=placed,
        out_specs=(P(None, "lat", "lon"), P(None, "lat", "lon"), P(None, "lat", "lon")),
        check_vma=False,
    )
```

```python
import functools

import jax
import jax.numpy as jnp
import ml_dtypes
import numpy as np
from jax import lax
from jax.experimental import pallas as pl
from jax.experimental.pallas import tpu as pltpu
from jax.sharding import PartitionSpec as P

NLON = 2560
NLAT = 1280
MMAX = 1280
F32 = jnp.float32
BF16 = jnp.bfloat16
STEPS = 64
CHUNKS = MMAX // STEPS
HALF = CHUNKS // 2
SLOTS = 4
TILES = 5
LANES = 128

cap_sine = 0.5
filter_width = 64.0
diffusion = 4.0
renorm_big = 2.0**64
renorm_step = 64.0


def split_np(values):
    values = np.asarray(values, np.float64).astype(np.float32)
    high = values.astype(ml_dtypes.bfloat16)
    low = (values - high.astype(np.float32)).astype(ml_dtypes.bfloat16)
    return high, low


def latitude_rows():
    rows = np.arange(NLAT // 2, dtype=np.float64)
    colatitude = (4.0 * rows + 3.0) * np.pi / (4.0 * NLAT + 2.0)
    shortfall = 1.0 / (8.0 * NLAT * NLAT) - 1.0 / (8.0 * NLAT * NLAT * NLAT)
    one_minus = shortfall + 2.0 * (1.0 - shortfall) * np.sin(0.5 * colatitude) ** 2
    one_plus = shortfall + 2.0 * (1.0 - shortfall) * np.cos(0.5 * colatitude) ** 2
    cosine = 0.5 * (one_plus - one_minus)
    sine = np.sqrt(one_minus * one_plus)
    weight = np.pi * sine / (NLAT + 0.5)
    log_sine = np.log2(sine)
    log_high = np.round(log_sine * 256.0) / 256.0
    log_low = log_sine - log_high
    table = np.stack([cosine, log_high, log_low, MMAX * sine / cap_sine, weight])
    lane = np.arange(NLAT // 2)
    order = 10 * (lane % 64) + lane // 64
    full = np.zeros((8, NLAT // 2), np.float32)
    full[:5] = table[:, order]
    return full


def sector_logs():
    order = np.arange(1, MMAX, dtype=np.float64)
    terms = np.log2((2.0 * order + 1.0) / (2.0 * order))
    return (-0.5 + 0.5 * np.concatenate([[0.0], np.cumsum(terms)])).astype(np.float32)


def gather_matrix():
    out = np.zeros((10, 3, 2, 2, 2, 256), np.float32)
    for u in range(10):
        for f in range(3):
            for q in range(2):
                for c in range(2):
                    for lev in range(2):
                        out[u, f, q, c, lev, q * 128 + c * 64 + (2 * f + lev) * 10 + u] = 1.0
    return out.reshape(240, 256).astype(ml_dtypes.bfloat16)


def fold_matrix():
    out = np.zeros((4, 128, 2, 128), np.float32)
    for src in range(64):
        out[0, src, :, src] = 1.0
        out[1, src, :, 64 + src] = 1.0
        out[2, 127 - src, 0, src] = 1.0
        out[2, 127 - src, 1, src] = -1.0
        out[3, 127 - src, 0, 64 + src] = 1.0
        out[3, 127 - src, 1, 64 + src] = -1.0
    return out.reshape(512, 256).astype(ml_dtypes.bfloat16)


def unfold_matrix():
    out = np.zeros((4, 64, 2, 128), np.float32)
    for row in range(64):
        out[0, row, :, row] = 1.0
        out[1, row, :, 64 + row] = 1.0
        out[2, row, 0, 63 - row] = 1.0
        out[2, row, 1, 63 - row] = -1.0
        out[3, row, 0, 127 - row] = 1.0
        out[3, row, 1, 127 - row] = -1.0
    return out.reshape(256, 256).astype(ml_dtypes.bfloat16)


def scatter_matrix():
    out = np.zeros((2, 2, 5, 8, 128), np.float32)
    for c in range(2):
        for h in range(2):
            for i in range(5):
                for f in range(3):
                    for lev in range(2):
                        out[c, h, i, 2 * f + lev, 40 * f + 4 * (5 * h + i) + 2 * c + lev] = 1.0
    return out.reshape(160, 128).astype(ml_dtypes.bfloat16)


def forward_matrix():
    angle = 2.0 * np.pi * (np.outer(np.arange(64), np.arange(128)) % 128) / 128.0
    table = np.concatenate([np.cos(angle), np.sin(angle)], axis=1) / NLON
    high, low = split_np(table)
    return np.concatenate([high, low], axis=0)


def inverse_matrix():
    angle = 2.0 * np.pi * (np.outer(np.arange(64), np.arange(128)) % 128) / 128.0
    cosine = np.cos(angle).reshape(2, 1, 32, 128)
    sine = np.sin(angle).reshape(2, 1, 32, 128)
    real_part = np.concatenate([cosine, sine], axis=-1)
    imag_part = np.concatenate([-sine, cosine], axis=-1)
    table = np.broadcast_to(np.stack([real_part, imag_part]), (2, 2, 4, 32, 256)).reshape(512, 256)
    high, low = split_np(table)
    return np.concatenate([high, low], axis=0)


def twiddles():
    angle = 2.0 * np.pi * np.outer(np.arange(20), np.arange(128)) / NLON
    return np.stack([np.cos(angle), np.sin(angle)], axis=1).reshape(40, 128).astype(np.float32)


def split(values):
    high = values.astype(BF16)
    return high, (values - high.astype(F32)).astype(BF16)


def dot(left, right):
    return lax.dot_general(left, right, (((1,), (0,)), ((), ())), preferred_element_type=F32)


def dot_t(left, right):
    return lax.dot_general(left, right, (((1,), (1,)), ((), ())), preferred_element_type=F32)


C1, C2 = float(np.cos(2 * np.pi / 5)), float(np.cos(4 * np.pi / 5))
S1, S2 = float(np.sin(2 * np.pi / 5)), float(np.sin(4 * np.pi / 5))


def pack_kernel(vort_hbm, div_hbm, height_hbm, out_ref, vort_ref, div_ref, height_ref, sem_ref):
    copies = [
        pltpu.make_async_copy(source, target, sem_ref.at[index])
        for index, (source, target) in enumerate(
            ((vort_hbm, vort_ref), (div_hbm, div_ref), (height_hbm, height_ref))
        )
    ]
    for copy in copies:
        copy.start()
    for b in range(4):
        out_ref[b, pl.ds(60, 4), :] = jnp.zeros((4, 640), F32)
    for f, ref in enumerate((vort_ref, div_ref, height_ref)):
        copies[f].wait()
        for b in range(4):
            for lev in range(2):
                out_ref[b, pl.ds((2 * f + lev) * 10, 10), :] = ref[lev, pl.ds(10 * b, 10), :]


def unpack_kernel(in_ref, vort_ref, div_ref, height_ref):
    for b in range(4):
        for f, ref in enumerate((vort_ref, div_ref, height_ref)):
            for lev in range(2):
                ref[lev, pl.ds(10 * b, 10), :] = in_ref[b, pl.ds((2 * f + lev) * 10, 10), :]


def forward_kernel(in_ref, twiddle_ref, table_ref, out_ref, z_ref):
    @pl.loop(0, 8)
    def _(group):
        rows = pl.ds(pl.multiple_of(group * 8, 8), 8)
        x = [in_ref[i2 // 5, rows, pl.ds((i2 % 5) * 128, 128)] for i2 in range(20)]
        parts = []
        for n4 in range(4):
            v = [x[(4 * n5 + 5 * n4) % 20] for n5 in range(5)]
            p1, p2 = v[1] + v[4], v[2] + v[3]
            q1, q2 = v[1] - v[4], v[2] - v[3]
            parts.append(
                (
                    (v[0] + p1 + p2, None),
                    (v[0] + C1 * p1 + C2 * p2, -(S1 * q1 + S2 * q2)),
                    (v[0] + C2 * p1 + C1 * p2, S1 * q2 - S2 * q1),
                )
            )
        y = {}
        zero = jnp.zeros_like(x[0])
        g = [parts[n4][0][0] for n4 in range(4)]
        y[0, 0] = (g[0] + g[2] + (g[1] + g[3]), zero)
        y[2, 0] = (g[0] + g[2] - (g[1] + g[3]), zero)
        y[1, 0] = (g[0] - g[2], g[3] - g[1])
        y[3, 0] = (g[0] - g[2], g[1] - g[3])
        for b5 in (1, 2):
            re = [parts[n4][b5][0] for n4 in range(4)]
            im = [parts[n4][b5][1] for n4 in range(4)]
            er, ei = re[0] + re[2], im[0] + im[2]
            odr, odi = re[1] + re[3], im[1] + im[3]
            dr, di = re[0] - re[2], im[0] - im[2]
            fr, fi = re[1] - re[3], im[1] - im[3]
            y[0, b5] = (er + odr, ei + odi)
            y[2, b5] = (er - odr, ei - odi)
            y[1, b5] = (dr + fi, di - fr)
            y[3, b5] = (dr - fi, di + fr)
        for b in range(20):
            if b % 5 <= 2:
                yr, yi = y[b % 4, b % 5]
            else:
                yr, yi = y[-b % 4, 5 - b % 5]
                yi = -yi
            tr = twiddle_ref[pl.ds(2 * b, 1), :]
            ti = twiddle_ref[pl.ds(2 * b + 1, 1), :]
            z_ref[b, rows, pl.ds(0, 128)] = yr * tr + yi * ti
            z_ref[b, rows, pl.ds(128, 128)] = yi * tr - yr * ti

    table = table_ref[...]
    for b in range(20):
        re = z_ref[b, :, pl.ds(0, 128)]
        im = z_ref[b, :, pl.ds(128, 128)]
        re_hi, re_lo = split(re)
        im_hi, im_lo = split(im)

        def both(real, imag):
            top = jnp.concatenate([real, imag], axis=1)
            return jnp.concatenate([top, jnp.concatenate([imag, -real], axis=1)], axis=0)

        first = dot_t(table, both(re_hi, im_hi))
        total = first[:64] + first[64:] + dot_t(table[:64], both(re_lo, im_lo))
        for h in range(2):
            out_ref[pl.ds((b // 5) * 32, 32), pl.ds((5 * h + b % 5) * 128, 128)] = total[
                h * 32 : (h + 1) * 32
            ]


def inverse_kernel(in_ref, scatter_ref, twiddle_ref, table_ref, out_ref, c_ref, z_ref):
    for part in range(4):
        for i in range(5):
            c_ref[part, i, pl.ds(56, 8), :] = jnp.zeros((8, LANES), F32)
    for u in range(10):
        high, low = split(in_ref[:, pl.ds(u * 128, 128)])
        moved = dot_t(scatter_ref[...], high) + dot_t(scatter_ref[...], low)
        for part in range(4):
            for i in range(5):
                start = (part * 5 + i) * 8
                c_ref[part, i, pl.ds(u, 6, stride=10), :] = moved[start : start + 6]
    table_hi = table_ref[pl.ds(0, 512), :]
    table_lo = table_ref[pl.ds(512, 512), :]
    lane_owner = (lax.broadcasted_iota(jnp.int32, (64, 512), 1) % 128) // 32
    for i in range(5):
        block = jnp.concatenate([c_ref[part, i] for part in range(4)], axis=1)
        for b1 in range(4):
            high, low = split(jnp.where(lane_owner == b1, block, 0.0))
            first = dot(jnp.concatenate([high, low], axis=0), table_hi)
            z_ref[5 * b1 + i] = first[:64] + first[64:] + dot(high, table_lo)

    @pl.loop(0, 8)
    def _(group):
        rows = pl.ds(pl.multiple_of(group * 8, 8), 8)
        z = {}
        for b in range(20):
            zr = z_ref[b, rows, pl.ds(0, 128)]
            zi = z_ref[b, rows, pl.ds(128, 128)]
            tr = twiddle_ref[pl.ds(2 * b, 1), :]
            ti = twiddle_ref[pl.ds(2 * b + 1, 1), :]
            z[b % 4, b % 5] = (zr * tr - zi * ti, zr * ti + zi * tr)
        parts = [[None] * 5 for _ in range(4)]
        for b5 in range(5):
            r0, i0 = z[0, b5]
            r1, i1 = z[1, b5]
            r2, i2 = z[2, b5]
            r3, i3 = z[3, b5]
            er, ei, dr, di = r0 + r2, i0 + i2, r0 - r2, i0 - i2
            sr, si, fr, fi = r1 + r3, i1 + i3, r1 - r3, i1 - i3
            parts[0][b5] = (er + sr, ei + si)
            parts[2][b5] = (er - sr, ei - si)
            parts[1][b5] = (dr - fi, di + fr)
            parts[3][b5] = (dr + fi, di - fr)
        for n4 in range(4):
            t = parts[n4]
            base = t[0][0]
            p1, p2 = t[1][0] + t[4][0], t[2][0] + t[3][0]
            q1, q2 = t[1][1] - t[4][1], t[2][1] - t[3][1]
            m1, m2 = base + C1 * p1 + C2 * p2, base + C2 * p1 + C1 * p2
            n1, n2 = S1 * q1 + S2 * q2, S2 * q1 - S1 * q2
            for n5, value in enumerate((base + p1 + p2, m1 - n1, m2 - n2, m2 + n2, m1 + n1)):
                i2 = (4 * n5 + 5 * n4) % 20
                out_ref[i2 // 5, rows, pl.ds((i2 % 5) * 128, 128)] = value


def table_kernel(phase, rank_ref, logs_ref, lat_ref, before_ref, table_ref, state_ref, coef_ref):
    rank = rank_ref[0]
    first = (rank % 32) * 20 + (rank // 32) * 5
    sub = lax.broadcasted_iota(jnp.int32, (8, LANES), 0)
    lane = lax.broadcasted_iota(jnp.int32, (8, LANES), 1)

    step_index = pl.program_id(0)

    @pl.when(step_index == 0)
    def _():
        fresh = (sub >= 5) | (phase == 0)
        shift = jnp.where(sub >= 5, 635 + 3 * phase, 0)
        wave = (first + sub + shift).astype(F32)
        logs = jnp.zeros((8, LANES), F32)
        for slot in range(8):
            offset = slot + (635 + 3 * phase if slot >= 5 else 0)
            offset = min(offset, 644)
            logs = jnp.where(sub == slot, logs_ref[first + offset], logs)
        for v in range(TILES):
            lanes = pl.ds(v * LANES, LANES)
            main = wave * lat_ref[pl.ds(1, 1), lanes]
            rest = wave * lat_ref[pl.ds(2, 1), lanes] + logs
            exponent = jnp.floor(main + rest)
            start = -jnp.exp2((main - exponent) + rest)
            state_ref[0, :, lanes] = jnp.where(fresh, 0.0, before_ref[0, :, lanes])
            state_ref[1, :, lanes] = jnp.where(fresh, start, before_ref[1, :, lanes])
            state_ref[2, :, lanes] = jnp.where(fresh, exponent, before_ref[2, :, lanes])

        def coefficients(turn, _):
            block = HALF * phase + turn
            step = block * STEPS + lane
            late = (sub >= 5) & (block >= CHUNKS // 2)
            wave_now = first + sub + jnp.where(sub >= 5, 635, 0) + jnp.where(late, 3, 0)
            excess = step - jnp.where(late, MMAX // 2, 0)
            live = (wave_now + excess < MMAX) & (jnp.logical_not(late) | (sub < 7))
            wave = wave_now.astype(F32)
            k = excess.astype(F32)
            degree = wave + k
            growth = jnp.sqrt((4.0 * degree * degree - 1.0) / jnp.maximum(k * (2.0 * wave + k), 1.0))
            backward = jnp.sqrt(
                jnp.maximum((k - 1.0) * (2.0 * wave + k - 1.0), 0.0)
                / jnp.maximum(4.0 * (degree - 1.0) * (degree - 1.0) - 1.0, 1.0)
            )
            start = excess == 0
            coef_ref[turn, 0] = jnp.where(live & jnp.logical_not(start), growth, 0.0)
            coef_ref[turn, 1] = jnp.where(live, jnp.where(start, 1.0, growth * backward), 0.0)
            return 0

        lax.fori_loop(0, HALF, coefficients, 0)

    def generate():
        newer, older, power, scale, cosine = [], [], [], [], []
        for v in range(TILES):
            lanes = pl.ds(v * LANES, LANES)
            newer.append(state_ref[0, :, lanes])
            older.append(state_ref[1, :, lanes])
            power.append(state_ref[2, :, lanes])
            cosine.append(jnp.broadcast_to(lat_ref[pl.ds(0, 1), lanes], (8, LANES)))
            scale.append(jnp.where(power[v] < -126.0, 0.0, jnp.exp2(power[v])))
        growth = coef_ref[step_index, 0]
        backward = coef_ref[step_index, 1]
        held = {}
        for t in range(STEPS):
            a = jnp.broadcast_to(growth[:, t : t + 1], (8, LANES))
            c = jnp.broadcast_to(backward[:, t : t + 1], (8, LANES))
            for v in range(TILES):
                value = (a * cosine[v]) * newer[v] - c * older[v]
                older[v], newer[v] = newer[v], value
                held[t, v] = value * scale[v]
            if t % 8 == 7:
                for v in range(TILES):
                    large = jnp.abs(newer[v]) > renorm_big
                    factor = jnp.where(large, 1.0 / renorm_big, 1.0)
                    newer[v] = newer[v] * factor
                    older[v] = older[v] * factor
                    power[v] = power[v] + jnp.where(large, renorm_step, 0.0)
                    scale[v] = jnp.where(power[v] < -126.0, 0.0, jnp.exp2(power[v]))
            if t % 4 == 3:
                rows = pl.ds((t // 4) * 16, 16)
                for v in range(TILES):
                    lanes = pl.ds(v * LANES, LANES)
                    for parity in range(2):
                        both = jnp.concatenate(
                            [held.pop((t - 3 + parity, v)), held.pop((t - 1 + parity, v))], axis=0
                        )
                        high, low = split(both)
                        table_ref[0, parity, 0, rows, lanes] = high
                        table_ref[0, parity, 1, rows, lanes] = low
        for v in range(TILES):
            lanes = pl.ds(v * LANES, LANES)
            state_ref[0, :, lanes] = newer[v]
            state_ref[1, :, lanes] = older[v]
            state_ref[2, :, lanes] = power[v]

    generate()


def legendre_kernel(
    rank_ref,
    geo_ref,
    in_ref,
    lat_ref,
    gather_ref,
    fold_ref,
    unfold_ref,
    early_ref,
    late_ref,
    out_ref,
    a_ref,
    x_ref,
    update0_ref,
    update1_ref,
    acc_ref,
    table_ref,
    sem_ref,
):
    rank = rank_ref[0]
    first = (rank % 32) * 20 + (rank // 32) * 5
    sub = lax.broadcasted_iota(jnp.int32, (8, LANES), 0)
    lane = lax.broadcasted_iota(jnp.int32, (8, LANES), 1)

    def fetch(block):
        slot = block % SLOTS

        @pl.when(block < HALF)
        def _():
            pltpu.make_async_copy(early_ref.at[block], table_ref.at[slot], sem_ref.at[slot]).start()

        @pl.when((block >= HALF) & (block < CHUNKS))
        def _():
            pltpu.make_async_copy(
                late_ref.at[block - HALF], table_ref.at[slot], sem_ref.at[slot]
            ).start()

    def arrived(block):
        slot = block % SLOTS
        pltpu.make_async_copy(early_ref.at[0], table_ref.at[slot], sem_ref.at[slot]).wait()

    for block in range(3):
        fetch(block)

    for u in range(10):
        a_ref[u, pl.ds(120, 8), :] = jnp.zeros((8, LANES), F32)
    for pair in range(5):
        high, low = split(in_ref[:, pl.ds(pair * 256, 256)])
        moved = dot_t(gather_ref[...], high) + dot_t(gather_ref[...], low)
        for u in range(10):
            for f in range(3):
                start = (u * 3 + f) * 8
                a_ref[u, pl.ds(f * 40 + pair * 8, 8), :] = moved[start : start + 8]

    for v in range(TILES):
        lanes = pl.ds(v * LANES, LANES)
        joined = jnp.concatenate(
            [a_ref[2 * v], a_ref[2 * v + 1], a_ref[9 - 2 * v], a_ref[8 - 2 * v]], axis=1
        )
        high, low = split(joined)
        folded = dot(high, fold_ref[...]) + dot(low, fold_ref[...])
        cut = lat_ref[pl.ds(3, 1), lanes]
        weight = lat_ref[pl.ds(4, 1), lanes]
        factors = []
        for pair in range(5):
            q = 2 * pair + sub // 4
            wave = first + q + jnp.where(q >= 5, 635, 0)
            excess = jnp.maximum(wave.astype(F32) - cut, 0.0) / filter_width
            doubling = jnp.where(wave == 0, 1.0, 2.0)
            factors.append(weight * jnp.exp(-0.5 * excess * excess) * doubling)
        factors = jnp.concatenate(factors * 3 + [jnp.zeros((8, LANES), F32)], axis=0)
        for parity in range(2):
            high, low = split(folded[:, parity * LANES : (parity + 1) * LANES] * factors)
            x_ref[parity, pl.ds(0, 128), lanes] = high
            x_ref[parity, pl.ds(128, 128), lanes] = low

    acc_ref[...] = jnp.zeros_like(acc_ref)
    geopot = jnp.where(sub % 2 == 0, geo_ref[0], geo_ref[1])

    def analyse(block, parity, update_ref):
        late = block >= CHUNKS // 2
        slot = lane % 8
        upper = slot >= 5
        wave = first + slot + jnp.where(upper, jnp.where(late, 638 - MMAX // 2, 635), 0)
        owner = slot + jnp.where(upper & late, 3, 0)
        both = dot_t(x_ref[parity], table_ref[block % SLOTS, parity, 0])
        spectral = both[:128] + both[128:] + dot_t(
            x_ref[parity, pl.ds(0, 128), :], table_ref[block % SLOTS, parity, 1]
        )
        halves = []
        for half in range(2):
            step = block * STEPS + 2 * (half * 16 + lane // 8) + parity
            degree = (wave + step).astype(F32)
            ratio = degree * (degree + 1.0) * (1.0 / (MMAX * MMAX))
            coupling = jnp.sqrt(ratio)
            damping = 1.0 / (1.0 + diffusion * ratio * ratio)
            shared = damping / (1.0 + geopot * ratio)
            cross = geopot * coupling
            part = spectral[:, half * LANES : (half + 1) * LANES]
            vort, div, height = [], [], []
            for pair in range(5):
                mine = owner == 2 * pair + sub // 4
                v_part = part[pair * 8 : pair * 8 + 8]
                d_part = part[40 + pair * 8 : 48 + pair * 8]
                h_part = part[80 + pair * 8 : 88 + pair * 8]
                mixed = jnp.where(mine, shared, 0.0)
                vort.append(jnp.where(mine, damping, 0.0) * v_part)
                div.append(mixed * (d_part + coupling * h_part))
                height.append(mixed * (h_part - cross * d_part))
            halves.append(
                jnp.concatenate(vort + div + height + [jnp.zeros((8, LANES), F32)], axis=0)
            )
        high, low = split(jnp.concatenate(halves, axis=1))
        update_ref[parity, pl.ds(0, 128), :] = high
        update_ref[parity, pl.ds(128, 128), :] = low

    def synthesise(block, parity, update_ref):
        both = dot(update_ref[parity], table_ref[block % SLOTS, parity, 0])
        rest = dot(update_ref[parity, pl.ds(0, 128), :], table_ref[block % SLOTS, parity, 1])
        acc_ref[parity] += both[:128] + both[128:] + rest

    arrived(0)
    for parity in range(2):
        analyse(0, parity, update0_ref)

    @pl.loop(0, CHUNKS // 2 - 1)
    def _(pair):
        for turn, (now, later) in enumerate(((update0_ref, update1_ref), (update1_ref, update0_ref))):
            block = 2 * pair + turn
            arrived(block + 1)
            fetch(block + 3)
            for parity in range(2):
                analyse(2 * pair + turn + 1, parity, later)
                synthesise(2 * pair + turn, parity, now)

    arrived(CHUNKS - 1)
    for parity in range(2):
        analyse(CHUNKS - 1, parity, update1_ref)
        synthesise(CHUNKS - 2, parity, update0_ref)
    for parity in range(2):
        synthesise(CHUNKS - 1, parity, update1_ref)

    for v in range(TILES):
        lanes = pl.ds(v * LANES, LANES)
        joined = jnp.concatenate([acc_ref[0, :, lanes], acc_ref[1, :, lanes]], axis=1)
        high, low = split(joined)
        moved = dot_t(unfold_ref[...], high) + dot_t(unfold_ref[...], low)
        for part, u in enumerate((2 * v, 2 * v + 1, 9 - 2 * v, 8 - 2 * v)):
            out_ref[pl.ds((part // 2) * 64, 64), pl.ds(u * LANES, LANES)] = moved[
                part * 64 : part * 64 + 64
            ]


VMEM = pl.BlockSpec(memory_space=pltpu.VMEM)
SMEM = pl.BlockSpec(memory_space=pltpu.SMEM)
HBM = pl.BlockSpec(memory_space=pltpu.HBM)


def call(kernel, outputs, specs, scratch, megabytes, flops, name, dtype=F32):
    shapes = tuple(jax.ShapeDtypeStruct(shape, dtype) for shape in outputs)
    single = len(shapes) == 1
    return pl.pallas_call(
        kernel,
        out_shape=shapes[0] if single else shapes,
        in_specs=specs,
        out_specs=VMEM if single else tuple(VMEM for _ in shapes),
        scratch_shapes=scratch,
        compiler_params=pltpu.CompilerParams(vmem_limit_bytes=megabytes << 20),
        cost_estimate=pl.CostEstimate(flops=flops, bytes_accessed=2 << 20, transcendentals=0),
        name=name,
    )


def table_call(phase, rank, logs, lat, before):
    def whole(*shape):
        return pl.BlockSpec(shape, lambda step: (0,) * len(shape))

    return pl.pallas_call(
        functools.partial(table_kernel, phase),
        grid=(HALF,),
        out_shape=(
            pltpu.HBM((HALF, 2, 2, 256, 640), BF16),
            jax.ShapeDtypeStruct((3, 8, 640), F32),
        ),
        in_specs=[SMEM, SMEM, whole(8, 640), whole(3, 8, 640)],
        out_specs=(
            pl.BlockSpec((1, 2, 2, 256, 640), lambda step: (step, 0, 0, 0, 0)),
            whole(3, 8, 640),
        ),
        scratch_shapes=[pltpu.VMEM((HALF, 2, 8, LANES), F32)],
        compiler_params=pltpu.CompilerParams(vmem_limit_bytes=12 << 20),
        cost_estimate=pl.CostEstimate(flops=1 << 32, bytes_accessed=13 << 20, transcendentals=0),
        name="table",
    )(rank, logs, lat, before)


def shards(vorticity, divergence, height, mean_geopot):
    rank = lax.axis_index("lat") * lax.axis_size("lon") + lax.axis_index("lon")
    rank = rank.astype(jnp.int32).reshape(1)
    twiddle = jnp.asarray(twiddles())
    packed = call(
        pack_kernel,
        [(4, 64, 640)],
        [HBM] * 3,
        [pltpu.VMEM((2, 40, 640), F32) for _ in range(3)] + [pltpu.SemaphoreType.DMA((3,))],
        8,
        1 << 20,
        "pack",
    )(
        *(pltpu.with_memory_space_constraint(x, pltpu.HBM) for x in (vorticity, divergence, height))
    )
    lat = jnp.asarray(latitude_rows())
    logs = jnp.asarray(sector_logs())
    early, state = table_call(0, rank, logs, lat, jnp.zeros((3, 8, 640), F32))
    sectors = lax.all_to_all(packed, "lon", split_axis=0, concat_axis=0, tiled=True)
    sectors, state = lax.optimization_barrier((sectors, state))
    spectrum = call(
        forward_kernel,
        [(128, 1280)],
        [VMEM] * 3,
        [pltpu.VMEM((20, 64, 256), F32)],
        16,
        1 << 28,
        "forward",
    )(sectors, twiddle, jnp.asarray(forward_matrix()))
    spectrum, state = lax.optimization_barrier((spectrum, state))
    late, _ = table_call(1, rank, logs, lat, state)
    columns = lax.all_to_all(spectrum, ("lat", "lon"), split_axis=0, concat_axis=0, tiled=True)
    synthesis = call(
        legendre_kernel,
        [(128, 1280)],
        [SMEM] * 2 + [VMEM] * 5 + [HBM] * 2,
        [
            pltpu.VMEM((10, 128, LANES), F32),
            pltpu.VMEM((2, 256, 640), BF16),
            pltpu.VMEM((2, 256, 256), BF16),
            pltpu.VMEM((2, 256, 256), BF16),
            pltpu.VMEM((2, 128, 640), F32),
            pltpu.VMEM((SLOTS, 2, 2, 256, 640), BF16),
            pltpu.SemaphoreType.DMA((SLOTS,)),
        ],
        20,
        1 << 33,
        "legendre",
    )(
        rank,
        mean_geopot,
        columns,
        lat,
        jnp.asarray(gather_matrix()),
        jnp.asarray(fold_matrix()),
        jnp.asarray(unfold_matrix()),
        pltpu.with_memory_space_constraint(early, pltpu.HBM),
        pltpu.with_memory_space_constraint(late, pltpu.HBM),
    )
    gathered = lax.all_to_all(synthesis, ("lat", "lon"), split_axis=0, concat_axis=0, tiled=True)
    result = call(
        inverse_kernel,
        [(4, 64, 640)],
        [VMEM] * 4,
        [pltpu.VMEM((4, 5, 64, LANES), F32), pltpu.VMEM((20, 64, 256), F32)],
        16,
        1 << 28,
        "inverse",
    )(gathered, jnp.asarray(scatter_matrix()), twiddle, jnp.asarray(inverse_matrix()))
    pieces = lax.all_to_all(result, "lon", split_axis=0, concat_axis=0, tiled=True)
    return call(unpack_kernel, [(2, 40, 640)] * 3, [VMEM], [], 8, 1 << 20, "unpack")(pieces)


def solution(mesh):
    placed = (P(None, "lat", "lon"), P(None, "lat", "lon"), P(None, "lat", "lon"), P())
    return jax.shard_map(
        shards,
        mesh=mesh,
        in_specs=placed,
        out_specs=(P(None, "lat", "lon"), P(None, "lat", "lon"), P(None, "lat", "lon")),
        check_vma=False,
    )
```

```python
import functools

import jax
import jax.numpy as jnp
import ml_dtypes
import numpy as np
from jax import lax
from jax.experimental import pallas as pl
from jax.experimental.pallas import tpu as pltpu
from jax.sharding import PartitionSpec as P

NLON = 2560
NLAT = 1280
MMAX = 1280
F32 = jnp.float32
BF16 = jnp.bfloat16
STEPS = 64
CHUNKS = MMAX // STEPS
HALF = CHUNKS // 2
SLOTS = 4
TILES = 5
LANES = 128

cap_sine = 0.5
filter_width = 64.0
diffusion = 4.0
renorm_big = 2.0**64
renorm_step = 64.0


def split_np(values):
    values = np.asarray(values, np.float64).astype(np.float32)
    high = values.astype(ml_dtypes.bfloat16)
    low = (values - high.astype(np.float32)).astype(ml_dtypes.bfloat16)
    return high, low


def latitude_rows():
    rows = np.arange(NLAT // 2, dtype=np.float64)
    colatitude = (4.0 * rows + 3.0) * np.pi / (4.0 * NLAT + 2.0)
    shortfall = 1.0 / (8.0 * NLAT * NLAT) - 1.0 / (8.0 * NLAT * NLAT * NLAT)
    one_minus = shortfall + 2.0 * (1.0 - shortfall) * np.sin(0.5 * colatitude) ** 2
    one_plus = shortfall + 2.0 * (1.0 - shortfall) * np.cos(0.5 * colatitude) ** 2
    cosine = 0.5 * (one_plus - one_minus)
    sine = np.sqrt(one_minus * one_plus)
    weight = np.pi * sine / (NLAT + 0.5)
    log_sine = np.log2(sine)
    log_high = np.round(log_sine * 256.0) / 256.0
    log_low = log_sine - log_high
    table = np.stack([cosine, log_high, log_low, MMAX * sine / cap_sine, weight])
    lane = np.arange(NLAT // 2)
    order = 10 * (lane % 64) + lane // 64
    full = np.zeros((8, NLAT // 2), np.float32)
    full[:5] = table[:, order]
    return full


def sector_logs():
    order = np.arange(1, MMAX, dtype=np.float64)
    terms = np.log2((2.0 * order + 1.0) / (2.0 * order))
    return (-0.5 + 0.5 * np.concatenate([[0.0], np.cumsum(terms)])).astype(np.float32)


def gather_matrix():
    out = np.zeros((10, 3, 2, 2, 2, 256), np.float32)
    for u in range(10):
        for f in range(3):
            for q in range(2):
                for c in range(2):
                    for lev in range(2):
                        out[u, f, q, c, lev, q * 128 + c * 64 + (2 * f + lev) * 10 + u] = 1.0
    return out.reshape(240, 256).astype(ml_dtypes.bfloat16)


def fold_matrix():
    out = np.zeros((4, 128, 2, 128), np.float32)
    for src in range(64):
        out[0, src, :, src] = 1.0
        out[1, src, :, 64 + src] = 1.0
        out[2, 127 - src, 0, src] = 1.0
        out[2, 127 - src, 1, src] = -1.0
        out[3, 127 - src, 0, 64 + src] = 1.0
        out[3, 127 - src, 1, 64 + src] = -1.0
    return out.reshape(512, 256).astype(ml_dtypes.bfloat16)


def unfold_matrix():
    out = np.zeros((4, 64, 2, 128), np.float32)
    for row in range(64):
        out[0, row, :, row] = 1.0
        out[1, row, :, 64 + row] = 1.0
        out[2, row, 0, 63 - row] = 1.0
        out[2, row, 1, 63 - row] = -1.0
        out[3, row, 0, 127 - row] = 1.0
        out[3, row, 1, 127 - row] = -1.0
    return out.reshape(256, 256).astype(ml_dtypes.bfloat16)


def scatter_matrix():
    out = np.zeros((2, 2, 5, 8, 128), np.float32)
    for c in range(2):
        for h in range(2):
            for i in range(5):
                for f in range(3):
                    for lev in range(2):
                        out[c, h, i, 2 * f + lev, 40 * f + 4 * (5 * h + i) + 2 * c + lev] = 1.0
    return out.reshape(160, 128).astype(ml_dtypes.bfloat16)


def forward_matrix():
    angle = 2.0 * np.pi * (np.outer(np.arange(64), np.arange(128)) % 128) / 128.0
    table = np.concatenate([np.cos(angle), np.sin(angle)], axis=1) / NLON
    high, low = split_np(table)
    return np.concatenate([high, low], axis=0)


def inverse_matrix():
    angle = 2.0 * np.pi * (np.outer(np.arange(64), np.arange(128)) % 128) / 128.0
    cosine = np.cos(angle).reshape(2, 1, 32, 128)
    sine = np.sin(angle).reshape(2, 1, 32, 128)
    real_part = np.concatenate([cosine, sine], axis=-1)
    imag_part = np.concatenate([-sine, cosine], axis=-1)
    table = np.broadcast_to(np.stack([real_part, imag_part]), (2, 2, 4, 32, 256)).reshape(512, 256)
    high, low = split_np(table)
    return np.concatenate([high, low], axis=0)


def twiddles():
    angle = 2.0 * np.pi * np.outer(np.arange(20), np.arange(128)) / NLON
    return np.stack([np.cos(angle), np.sin(angle)], axis=1).reshape(40, 128).astype(np.float32)


def split(values):
    high = values.astype(BF16)
    return high, (values - high.astype(F32)).astype(BF16)


def dot(left, right):
    return lax.dot_general(left, right, (((1,), (0,)), ((), ())), preferred_element_type=F32)


def dot_t(left, right):
    return lax.dot_general(left, right, (((1,), (1,)), ((), ())), preferred_element_type=F32)


C1, C2 = float(np.cos(2 * np.pi / 5)), float(np.cos(4 * np.pi / 5))
S1, S2 = float(np.sin(2 * np.pi / 5)), float(np.sin(4 * np.pi / 5))


def pack_kernel(
    rank_ref,
    logs_hbm,
    lat_hbm,
    vort_hbm,
    div_hbm,
    height_hbm,
    out_ref,
    start_ref,
    lat_ref,
    vort_ref,
    div_ref,
    height_ref,
    logs_ref,
    sem_ref,
):
    copies = [
        pltpu.make_async_copy(source, target, sem_ref.at[index])
        for index, (source, target) in enumerate(
            (
                (vort_hbm, vort_ref),
                (div_hbm, div_ref),
                (height_hbm, height_ref),
                (logs_hbm, logs_ref),
                (lat_hbm, lat_ref),
            )
        )
    ]
    for copy in copies:
        copy.start()
    for b in range(4):
        out_ref[b, pl.ds(60, 4), :] = jnp.zeros((4, 640), F32)
    for f, ref in enumerate((vort_ref, div_ref, height_ref)):
        copies[f].wait()
        for b in range(4):
            for lev in range(2):
                out_ref[b, pl.ds((2 * f + lev) * 10, 10), :] = ref[lev, pl.ds(10 * b, 10), :]
    copies[3].wait()
    copies[4].wait()
    rank = rank_ref[0]
    first = (rank % 32) * 20 + (rank // 32) * 5
    sub = lax.broadcasted_iota(jnp.int32, (8, LANES), 0)
    for phase in range(2):
        logs = jnp.zeros((8, LANES), F32)
        for slot in range(8):
            offset = min(slot + (635 + 3 * phase if slot >= 5 else 0), 644)
            logs = jnp.where(sub == slot, logs_ref[first + offset], logs)
        start_ref[phase] = logs


def unpack_kernel(
    rank_ref, in0_ref, in1_ref, in2_ref, in3_ref, vort_ref, div_ref, height_ref
):
    pieces = (in0_ref, in1_ref, in2_ref, in3_ref)

    def place(lon):
        for b in range(4):
            for f, ref in enumerate((vort_ref, div_ref, height_ref)):
                for lev in range(2):
                    ref[lev, pl.ds(10 * b, 10), :] = pieces[(lon - b) % 4][
                        pl.ds((2 * f + lev) * 10, 10), :
                    ]

    for lon in range(4):
        pl.when(rank_ref[0] % 4 == lon)(functools.partial(place, lon))


def forward_kernel(in_ref, twiddle_ref, table_ref, out_ref, z_ref):
    @pl.loop(0, 8)
    def _(group):
        rows = pl.ds(pl.multiple_of(group * 8, 8), 8)
        x = [in_ref[i2 // 5, rows, pl.ds((i2 % 5) * 128, 128)] for i2 in range(20)]
        parts = []
        for n4 in range(4):
            v = [x[(4 * n5 + 5 * n4) % 20] for n5 in range(5)]
            p1, p2 = v[1] + v[4], v[2] + v[3]
            q1, q2 = v[1] - v[4], v[2] - v[3]
            parts.append(
                (
                    (v[0] + p1 + p2, None),
                    (v[0] + C1 * p1 + C2 * p2, -(S1 * q1 + S2 * q2)),
                    (v[0] + C2 * p1 + C1 * p2, S1 * q2 - S2 * q1),
                )
            )
        y = {}
        zero = jnp.zeros_like(x[0])
        g = [parts[n4][0][0] for n4 in range(4)]
        y[0, 0] = (g[0] + g[2] + (g[1] + g[3]), zero)
        y[2, 0] = (g[0] + g[2] - (g[1] + g[3]), zero)
        y[1, 0] = (g[0] - g[2], g[3] - g[1])
        y[3, 0] = (g[0] - g[2], g[1] - g[3])
        for b5 in (1, 2):
            re = [parts[n4][b5][0] for n4 in range(4)]
            im = [parts[n4][b5][1] for n4 in range(4)]
            er, ei = re[0] + re[2], im[0] + im[2]
            odr, odi = re[1] + re[3], im[1] + im[3]
            dr, di = re[0] - re[2], im[0] - im[2]
            fr, fi = re[1] - re[3], im[1] - im[3]
            y[0, b5] = (er + odr, ei + odi)
            y[2, b5] = (er - odr, ei - odi)
            y[1, b5] = (dr + fi, di - fr)
            y[3, b5] = (dr - fi, di + fr)
        for b in range(20):
            if b % 5 <= 2:
                yr, yi = y[b % 4, b % 5]
            else:
                yr, yi = y[-b % 4, 5 - b % 5]
                yi = -yi
            tr = twiddle_ref[pl.ds(2 * b, 1), :]
            ti = twiddle_ref[pl.ds(2 * b + 1, 1), :]
            z_ref[b, rows, pl.ds(0, 128)] = yr * tr + yi * ti
            z_ref[b, rows, pl.ds(128, 128)] = yi * tr - yr * ti

    table = table_ref[...]
    for b in range(20):
        re = z_ref[b, :, pl.ds(0, 128)]
        im = z_ref[b, :, pl.ds(128, 128)]
        re_hi, re_lo = split(re)
        im_hi, im_lo = split(im)

        def both(real, imag):
            top = jnp.concatenate([real, imag], axis=1)
            return jnp.concatenate([top, jnp.concatenate([imag, -real], axis=1)], axis=0)

        first = dot_t(table, both(re_hi, im_hi))
        total = first[:64] + first[64:] + dot_t(table[:64], both(re_lo, im_lo))
        for h in range(2):
            out_ref[pl.ds((b // 5) * 32, 32), pl.ds((5 * h + b % 5) * 128, 128)] = total[
                h * 32 : (h + 1) * 32
            ]


def inverse_kernel(
    rank_ref,
    in_ref,
    scatter_ref,
    twiddle_ref,
    table_ref,
    out0_ref,
    out1_ref,
    out2_ref,
    out3_ref,
    c_ref,
    z_ref,
    out_ref,
):
    for part in range(4):
        for i in range(5):
            c_ref[part, i, pl.ds(56, 8), :] = jnp.zeros((8, LANES), F32)
    for u in range(10):
        high, low = split(in_ref[:, pl.ds(u * 128, 128)])
        moved = dot_t(scatter_ref[...], high) + dot_t(scatter_ref[...], low)
        for part in range(4):
            for i in range(5):
                start = (part * 5 + i) * 8
                c_ref[part, i, pl.ds(u, 6, stride=10), :] = moved[start : start + 6]
    table_hi = table_ref[pl.ds(0, 512), :]
    table_lo = table_ref[pl.ds(512, 512), :]
    lane_owner = (lax.broadcasted_iota(jnp.int32, (64, 512), 1) % 128) // 32
    for i in range(5):
        block = jnp.concatenate([c_ref[part, i] for part in range(4)], axis=1)
        for b1 in range(4):
            high, low = split(jnp.where(lane_owner == b1, block, 0.0))
            first = dot(jnp.concatenate([high, low], axis=0), table_hi)
            z_ref[5 * b1 + i] = first[:64] + first[64:] + dot(high, table_lo)

    @pl.loop(0, 8)
    def _(group):
        rows = pl.ds(pl.multiple_of(group * 8, 8), 8)
        z = {}
        for b in range(20):
            zr = z_ref[b, rows, pl.ds(0, 128)]
            zi = z_ref[b, rows, pl.ds(128, 128)]
            tr = twiddle_ref[pl.ds(2 * b, 1), :]
            ti = twiddle_ref[pl.ds(2 * b + 1, 1), :]
            z[b % 4, b % 5] = (zr * tr - zi * ti, zr * ti + zi * tr)
        parts = [[None] * 5 for _ in range(4)]
        for b5 in range(5):
            r0, i0 = z[0, b5]
            r1, i1 = z[1, b5]
            r2, i2 = z[2, b5]
            r3, i3 = z[3, b5]
            er, ei, dr, di = r0 + r2, i0 + i2, r0 - r2, i0 - i2
            sr, si, fr, fi = r1 + r3, i1 + i3, r1 - r3, i1 - i3
            parts[0][b5] = (er + sr, ei + si)
            parts[2][b5] = (er - sr, ei - si)
            parts[1][b5] = (dr - fi, di + fr)
            parts[3][b5] = (dr + fi, di - fr)
        for n4 in range(4):
            t = parts[n4]
            base = t[0][0]
            p1, p2 = t[1][0] + t[4][0], t[2][0] + t[3][0]
            q1, q2 = t[1][1] - t[4][1], t[2][1] - t[3][1]
            m1, m2 = base + C1 * p1 + C2 * p2, base + C2 * p1 + C1 * p2
            n1, n2 = S1 * q1 + S2 * q2, S2 * q1 - S1 * q2
            for n5, value in enumerate((base + p1 + p2, m1 - n1, m2 - n2, m2 + n2, m1 + n1)):
                i2 = (4 * n5 + 5 * n4) % 20
                out_ref[i2 // 5, rows, pl.ds((i2 % 5) * 128, 128)] = value

    for shift, piece_ref in enumerate((out0_ref, out1_ref, out2_ref, out3_ref)):
        piece_ref[...] = out_ref[(rank_ref[0] + shift) % 4]


def table_kernel(
    phase,
    rank_ref,
    logs_ref,
    lat_ref,
    before_ref,
    table_ref,
    state_ref,
    coef_ref,
    buf_ref,
    sem_ref,
):
    rank = rank_ref[0]
    first = (rank % 32) * 20 + (rank // 32) * 5
    sub = lax.broadcasted_iota(jnp.int32, (8, LANES), 0)
    lane = lax.broadcasted_iota(jnp.int32, (8, LANES), 1)

    step_index = pl.program_id(0)

    @pl.when(step_index == 0)
    def _():
        fresh = (sub >= 5) | (phase == 0)
        shift = jnp.where(sub >= 5, 635 + 3 * phase, 0)
        wave = (first + sub + shift).astype(F32)
        logs = logs_ref[phase]
        for v in range(TILES):
            lanes = pl.ds(v * LANES, LANES)
            main = wave * lat_ref[pl.ds(1, 1), lanes]
            rest = wave * lat_ref[pl.ds(2, 1), lanes] + logs
            exponent = jnp.floor(main + rest)
            start = -jnp.exp2((main - exponent) + rest)
            state_ref[0, :, lanes] = jnp.where(fresh, 0.0, before_ref[0, :, lanes])
            state_ref[1, :, lanes] = jnp.where(fresh, start, before_ref[1, :, lanes])
            state_ref[2, :, lanes] = jnp.where(fresh, exponent, before_ref[2, :, lanes])

        def coefficients(turn, _):
            block = HALF * phase + turn
            step = block * STEPS + lane
            late = (sub >= 5) & (block >= CHUNKS // 2)
            wave_now = first + sub + jnp.where(sub >= 5, 635, 0) + jnp.where(late, 3, 0)
            excess = step - jnp.where(late, MMAX // 2, 0)
            live = (wave_now + excess < MMAX) & (jnp.logical_not(late) | (sub < 7))
            wave = wave_now.astype(F32)
            k = excess.astype(F32)
            degree = wave + k
            growth = jnp.sqrt((4.0 * degree * degree - 1.0) / jnp.maximum(k * (2.0 * wave + k), 1.0))
            backward = jnp.sqrt(
                jnp.maximum((k - 1.0) * (2.0 * wave + k - 1.0), 0.0)
                / jnp.maximum(4.0 * (degree - 1.0) * (degree - 1.0) - 1.0, 1.0)
            )
            start = excess == 0
            coef_ref[turn, 0] = jnp.where(live & jnp.logical_not(start), growth, 0.0)
            coef_ref[turn, 1] = jnp.where(live, jnp.where(start, 1.0, growth * backward), 0.0)
            return 0

        lax.fori_loop(0, HALF, coefficients, 0)

    slot = step_index % 2

    def copies(step):
        return [
            pltpu.make_async_copy(
                buf_ref.at[step % 2, part // 2, part % 2],
                table_ref.at[step, part // 2, part % 2],
                sem_ref.at[step % 2, part],
            )
            for part in range(4)
        ]

    def finish(step):
        for copy in copies(step):
            copy.wait()

    def generate():
        newer, older, power, scale, cosine = [], [], [], [], []
        for v in range(TILES):
            lanes = pl.ds(v * LANES, LANES)
            newer.append(state_ref[0, :, lanes])
            older.append(state_ref[1, :, lanes])
            power.append(state_ref[2, :, lanes])
            cosine.append(jnp.broadcast_to(lat_ref[pl.ds(0, 1), lanes], (8, LANES)))
            scale.append(jnp.where(power[v] < -126.0, 0.0, jnp.exp2(power[v])))
        growth = coef_ref[step_index, 0]
        backward = coef_ref[step_index, 1]
        held = {}
        for t in range(STEPS):
            a = jnp.broadcast_to(growth[:, t : t + 1], (8, LANES))
            c = jnp.broadcast_to(backward[:, t : t + 1], (8, LANES))
            for v in range(TILES):
                value = (a * cosine[v]) * newer[v] - c * older[v]
                older[v], newer[v] = newer[v], value
                held[t, v] = value * scale[v]
            if t % 8 == 7:
                for v in range(TILES):
                    large = jnp.abs(newer[v]) > renorm_big
                    factor = jnp.where(large, 1.0 / renorm_big, 1.0)
                    newer[v] = newer[v] * factor
                    older[v] = older[v] * factor
                    power[v] = power[v] + jnp.where(large, renorm_step, 0.0)
                    scale[v] = jnp.where(power[v] < -126.0, 0.0, jnp.exp2(power[v]))
            if t % 4 == 3:
                rows = pl.ds((t // 4) * 16, 16)
                for v in range(TILES):
                    lanes = pl.ds(v * LANES, LANES)
                    for parity in range(2):
                        both = jnp.concatenate(
                            [held.pop((t - 3 + parity, v)), held.pop((t - 1 + parity, v))], axis=0
                        )
                        high, low = split(both)
                        buf_ref[slot, parity, 0, rows, lanes] = high
                        buf_ref[slot, parity, 1, rows, lanes] = low
        for v in range(TILES):
            lanes = pl.ds(v * LANES, LANES)
            state_ref[0, :, lanes] = newer[v]
            state_ref[1, :, lanes] = older[v]
            state_ref[2, :, lanes] = power[v]

    pl.when(step_index >= 2)(lambda: finish(step_index - 2))
    generate()
    for copy in copies(step_index):
        copy.start()

    @pl.when(step_index == HALF - 1)
    def _():
        finish(HALF - 2)
        finish(HALF - 1)


def legendre_kernel(
    rank_ref,
    geo_ref,
    in_ref,
    lat_ref,
    gather_ref,
    fold_ref,
    unfold_ref,
    early_ref,
    late_ref,
    out_ref,
    a_ref,
    x_ref,
    update0_ref,
    update1_ref,
    acc_ref,
    table_ref,
    sem_ref,
):
    rank = rank_ref[0]
    first = (rank % 32) * 20 + (rank // 32) * 5
    sub = lax.broadcasted_iota(jnp.int32, (8, LANES), 0)
    lane = lax.broadcasted_iota(jnp.int32, (8, LANES), 1)

    def pieces(source_ref, index, slot):
        return [
            pltpu.make_async_copy(
                source_ref.at[index, part // 2, part % 2],
                table_ref.at[slot, part // 2, part % 2],
                sem_ref.at[slot, part],
            )
            for part in range(4)
        ]

    def fetch(block):
        slot = block % SLOTS

        @pl.when(block < HALF)
        def _():
            for copy in pieces(early_ref, block, slot):
                copy.start()

        @pl.when((block >= HALF) & (block < CHUNKS))
        def _():
            for copy in pieces(late_ref, block - HALF, slot):
                copy.start()

    def arrived(block):
        for copy in pieces(early_ref, 0, block % SLOTS):
            copy.wait()

    for block in range(3):
        fetch(block)

    for u in range(10):
        a_ref[u, pl.ds(120, 8), :] = jnp.zeros((8, LANES), F32)
    for pair in range(5):
        high, low = split(in_ref[:, pl.ds(pair * 256, 256)])
        moved = dot_t(gather_ref[...], high) + dot_t(gather_ref[...], low)
        for u in range(10):
            for f in range(3):
                start = (u * 3 + f) * 8
                a_ref[u, pl.ds(f * 40 + pair * 8, 8), :] = moved[start : start + 8]

    for v in range(TILES):
        lanes = pl.ds(v * LANES, LANES)
        joined = jnp.concatenate(
            [a_ref[2 * v], a_ref[2 * v + 1], a_ref[9 - 2 * v], a_ref[8 - 2 * v]], axis=1
        )
        high, low = split(joined)
        folded = dot(high, fold_ref[...]) + dot(low, fold_ref[...])
        cut = lat_ref[pl.ds(3, 1), lanes]
        weight = lat_ref[pl.ds(4, 1), lanes]
        factors = []
        for pair in range(5):
            q = 2 * pair + sub // 4
            wave = first + q + jnp.where(q >= 5, 635, 0)
            excess = jnp.maximum(wave.astype(F32) - cut, 0.0) / filter_width
            doubling = jnp.where(wave == 0, 1.0, 2.0)
            factors.append(weight * jnp.exp(-0.5 * excess * excess) * doubling)
        factors = jnp.concatenate(factors * 3 + [jnp.zeros((8, LANES), F32)], axis=0)
        for parity in range(2):
            high, low = split(folded[:, parity * LANES : (parity + 1) * LANES] * factors)
            x_ref[parity, pl.ds(0, 128), lanes] = high
            x_ref[parity, pl.ds(128, 128), lanes] = low

    acc_ref[...] = jnp.zeros_like(acc_ref)
    geopot = jnp.where(sub % 2 == 0, geo_ref[0], geo_ref[1])

    def analyse(block, parity, update_ref):
        late = block >= CHUNKS // 2
        slot = lane % 8
        upper = slot >= 5
        wave = first + slot + jnp.where(upper, jnp.where(late, 638 - MMAX // 2, 635), 0)
        owner = slot + jnp.where(upper & late, 3, 0)
        both = dot_t(x_ref[parity], table_ref[block % SLOTS, parity, 0])
        spectral = both[:128] + both[128:] + dot_t(
            x_ref[parity, pl.ds(0, 128), :], table_ref[block % SLOTS, parity, 1]
        )
        halves = []
        for half in range(2):
            step = block * STEPS + 2 * (half * 16 + lane // 8) + parity
            degree = (wave + step).astype(F32)
            ratio = degree * (degree + 1.0) * (1.0 / (MMAX * MMAX))
            coupling = jnp.sqrt(ratio)
            damping = 1.0 / (1.0 + diffusion * ratio * ratio)
            shared = damping / (1.0 + geopot * ratio)
            cross = geopot * coupling
            part = spectral[:, half * LANES : (half + 1) * LANES]
            vort, div, height = [], [], []
            for pair in range(5):
                mine = owner == 2 * pair + sub // 4
                v_part = part[pair * 8 : pair * 8 + 8]
                d_part = part[40 + pair * 8 : 48 + pair * 8]
                h_part = part[80 + pair * 8 : 88 + pair * 8]
                mixed = jnp.where(mine, shared, 0.0)
                vort.append(jnp.where(mine, damping, 0.0) * v_part)
                div.append(mixed * (d_part + coupling * h_part))
                height.append(mixed * (h_part - cross * d_part))
            halves.append(
                jnp.concatenate(vort + div + height + [jnp.zeros((8, LANES), F32)], axis=0)
            )
        high, low = split(jnp.concatenate(halves, axis=1))
        update_ref[parity, pl.ds(0, 128), :] = high
        update_ref[parity, pl.ds(128, 128), :] = low

    def synthesise(block, parity, update_ref):
        both = dot(update_ref[parity], table_ref[block % SLOTS, parity, 0])
        rest = dot(update_ref[parity, pl.ds(0, 128), :], table_ref[block % SLOTS, parity, 1])
        acc_ref[parity] += both[:128] + both[128:] + rest

    arrived(0)
    for parity in range(2):
        analyse(0, parity, update0_ref)

    @pl.loop(0, CHUNKS // 2 - 1)
    def _(pair):
        for turn, (now, later) in enumerate(((update0_ref, update1_ref), (update1_ref, update0_ref))):
            block = 2 * pair + turn
            arrived(block + 1)
            fetch(block + 3)
            for parity in range(2):
                analyse(2 * pair + turn + 1, parity, later)
                synthesise(2 * pair + turn, parity, now)

    arrived(CHUNKS - 1)
    for parity in range(2):
        analyse(CHUNKS - 1, parity, update1_ref)
        synthesise(CHUNKS - 2, parity, update0_ref)
    for parity in range(2):
        synthesise(CHUNKS - 1, parity, update1_ref)

    for v in range(TILES):
        lanes = pl.ds(v * LANES, LANES)
        joined = jnp.concatenate([acc_ref[0, :, lanes], acc_ref[1, :, lanes]], axis=1)
        high, low = split(joined)
        moved = dot_t(unfold_ref[...], high) + dot_t(unfold_ref[...], low)
        for part, u in enumerate((2 * v, 2 * v + 1, 9 - 2 * v, 8 - 2 * v)):
            out_ref[pl.ds(64 - (part // 2) * 64, 64), pl.ds(u * LANES, LANES)] = moved[
                part * 64 : part * 64 + 64
            ]


VMEM = pl.BlockSpec(memory_space=pltpu.VMEM)
SMEM = pl.BlockSpec(memory_space=pltpu.SMEM)
HBM = pl.BlockSpec(memory_space=pltpu.HBM)


def call(kernel, outputs, specs, scratch, megabytes, flops, name, dtype=F32):
    shapes = tuple(jax.ShapeDtypeStruct(shape, dtype) for shape in outputs)
    single = len(shapes) == 1
    return pl.pallas_call(
        kernel,
        out_shape=shapes[0] if single else shapes,
        in_specs=specs,
        out_specs=VMEM if single else tuple(VMEM for _ in shapes),
        scratch_shapes=scratch,
        compiler_params=pltpu.CompilerParams(vmem_limit_bytes=megabytes << 20),
        cost_estimate=pl.CostEstimate(flops=flops, bytes_accessed=2 << 20, transcendentals=0),
        name=name,
    )


def table_call(phase, rank, logs, lat, before):
    def whole(*shape):
        return pl.BlockSpec(shape, lambda step: (0,) * len(shape))

    return pl.pallas_call(
        functools.partial(table_kernel, phase),
        grid=(HALF,),
        out_shape=(
            pltpu.HBM((HALF, 2, 2, 256, 640), BF16),
            jax.ShapeDtypeStruct((3, 8, 640), F32),
        ),
        in_specs=[SMEM, whole(2, 8, LANES), whole(8, 640), whole(3, 8, 640)],
        out_specs=(
            HBM,
            whole(3, 8, 640),
        ),
        scratch_shapes=[
            pltpu.VMEM((HALF, 2, 8, LANES), F32),
            pltpu.VMEM((2, 2, 2, 256, 640), BF16),
            pltpu.SemaphoreType.DMA((2, 4)),
        ],
        compiler_params=pltpu.CompilerParams(vmem_limit_bytes=12 << 20),
        cost_estimate=pl.CostEstimate(flops=1 << 32, bytes_accessed=13 << 20, transcendentals=0),
        name="table",
    )(rank, logs, lat, before)


def shards(vorticity, divergence, height, mean_geopot):
    rank = lax.axis_index("lat") * lax.axis_size("lon") + lax.axis_index("lon")
    rank = rank.astype(jnp.int32).reshape(1)
    twiddle = jnp.asarray(twiddles())
    sources = (jnp.asarray(sector_logs()), jnp.asarray(latitude_rows()), vorticity, divergence, height)
    packed, logs, lat = call(
        pack_kernel,
        [(4, 64, 640), (2, 8, LANES), (8, 640)],
        [SMEM] + [HBM] * 5,
        [pltpu.VMEM((2, 40, 640), F32) for _ in range(3)]
        + [pltpu.SMEM((MMAX,), F32), pltpu.SemaphoreType.DMA((5,))],
        8,
        1 << 20,
        "pack",
    )(rank, *(pltpu.with_memory_space_constraint(x, pltpu.HBM) for x in sources))
    early, state = table_call(0, rank, logs, lat, jnp.zeros((3, 8, 640), F32))
    sectors = lax.all_to_all(packed, "lon", split_axis=0, concat_axis=0, tiled=True)
    sectors, state = lax.optimization_barrier((sectors, state))
    spectrum = call(
        forward_kernel,
        [(128, 1280)],
        [VMEM] * 3,
        [pltpu.VMEM((20, 64, 256), F32)],
        16,
        1 << 28,
        "forward",
    )(sectors, twiddle, jnp.asarray(forward_matrix()))
    spectrum, state = lax.optimization_barrier((spectrum, state))
    late, _ = table_call(1, rank, logs, lat, state)
    columns = lax.all_to_all(spectrum, ("lat", "lon"), split_axis=0, concat_axis=0, tiled=True)
    synthesis = call(
        legendre_kernel,
        [(128, 1280)],
        [SMEM] * 2 + [VMEM] * 5 + [HBM] * 2,
        [
            pltpu.VMEM((10, 128, LANES), F32),
            pltpu.VMEM((2, 256, 640), BF16),
            pltpu.VMEM((2, 256, 256), BF16),
            pltpu.VMEM((2, 256, 256), BF16),
            pltpu.VMEM((2, 128, 640), F32),
            pltpu.VMEM((SLOTS, 2, 2, 256, 640), BF16),
            pltpu.SemaphoreType.DMA((SLOTS, 4)),
        ],
        20,
        1 << 33,
        "legendre",
    )(
        rank,
        mean_geopot,
        columns,
        lat,
        jnp.asarray(gather_matrix()),
        jnp.asarray(fold_matrix()),
        jnp.asarray(unfold_matrix()),
        pltpu.with_memory_space_constraint(early, pltpu.HBM),
        pltpu.with_memory_space_constraint(late, pltpu.HBM),
    )
    gathered = lax.all_to_all(synthesis, ("lat", "lon"), split_axis=0, concat_axis=0, tiled=True)
    result = call(
        inverse_kernel,
        [(64, 640)] * 4,
        [SMEM] + [VMEM] * 4,
        [
            pltpu.VMEM((4, 5, 64, LANES), F32),
            pltpu.VMEM((20, 64, 256), F32),
            pltpu.VMEM((4, 64, 640), F32),
        ],
        16,
        1 << 28,
        "inverse",
    )(rank, gathered, jnp.asarray(scatter_matrix()), twiddle, jnp.asarray(inverse_matrix()))
    n_lat = lax.axis_size("lat")
    n_lon = lax.axis_size("lon")
    pieces = []
    for shift, piece in enumerate(result):
        pairs = [
            (lat_at * n_lon + lon_at, (lat_at ^ 16) * n_lon + (lon_at + shift) % n_lon)
            for lat_at in range(n_lat)
            for lon_at in range(n_lon)
        ]
        pieces.append(lax.ppermute(piece, ("lat", "lon"), pairs))
    return call(unpack_kernel, [(2, 40, 640)] * 3, [SMEM] + [VMEM] * 4, [], 8, 1 << 20, "unpack")(
        rank, *pieces
    )


def solution(mesh):
    placed = (P(None, "lat", "lon"), P(None, "lat", "lon"), P(None, "lat", "lon"), P())
    return jax.shard_map(
        shards,
        mesh=mesh,
        in_specs=placed,
        out_specs=(P(None, "lat", "lon"), P(None, "lat", "lon"), P(None, "lat", "lon")),
        check_vma=False,
    )
```

```python
import functools

import jax
import jax.numpy as jnp
import ml_dtypes
import numpy as np
from jax import lax
from jax.experimental import pallas as pl
from jax.experimental.pallas import tpu as pltpu
from jax.sharding import PartitionSpec as P

NLON = 2560
NLAT = 1280
MMAX = 1280
F32 = jnp.float32
BF16 = jnp.bfloat16
STEPS = 64
CHUNKS = MMAX // STEPS
HALF = CHUNKS // 2
SLOTS = 4
TILES = 5
LANES = 128

cap_sine = 0.5
filter_width = 64.0
diffusion = 4.0
renorm_big = 2.0**64
renorm_step = 64.0


def split_np(values):
    values = np.asarray(values, np.float64).astype(np.float32)
    high = values.astype(ml_dtypes.bfloat16)
    low = (values - high.astype(np.float32)).astype(ml_dtypes.bfloat16)
    return high, low


def latitude_rows():
    rows = np.arange(NLAT // 2, dtype=np.float64)
    colatitude = (4.0 * rows + 3.0) * np.pi / (4.0 * NLAT + 2.0)
    shortfall = 1.0 / (8.0 * NLAT * NLAT) - 1.0 / (8.0 * NLAT * NLAT * NLAT)
    one_minus = shortfall + 2.0 * (1.0 - shortfall) * np.sin(0.5 * colatitude) ** 2
    one_plus = shortfall + 2.0 * (1.0 - shortfall) * np.cos(0.5 * colatitude) ** 2
    cosine = 0.5 * (one_plus - one_minus)
    sine = np.sqrt(one_minus * one_plus)
    weight = np.pi * sine / (NLAT + 0.5)
    log_sine = np.log2(sine)
    log_high = np.round(log_sine * 256.0) / 256.0
    log_low = log_sine - log_high
    table = np.stack([cosine, log_high, log_low, MMAX * sine / cap_sine, weight])
    lane = np.arange(NLAT // 2)
    order = 10 * (lane % 64) + lane // 64
    full = np.zeros((8, NLAT // 2), np.float32)
    full[:5] = table[:, order]
    return full


def sector_logs():
    order = np.arange(1, MMAX, dtype=np.float64)
    terms = np.log2((2.0 * order + 1.0) / (2.0 * order))
    return (-0.5 + 0.5 * np.concatenate([[0.0], np.cumsum(terms)])).astype(np.float32)


def gather_matrix():
    out = np.zeros((10, 3, 2, 2, 2, 256), np.float32)
    for u in range(10):
        for f in range(3):
            for q in range(2):
                for c in range(2):
                    for lev in range(2):
                        out[u, f, q, c, lev, q * 128 + c * 64 + (2 * f + lev) * 10 + u] = 1.0
    return out.reshape(240, 256).astype(ml_dtypes.bfloat16)


def fold_matrix():
    out = np.zeros((4, 128, 2, 128), np.float32)
    for src in range(64):
        out[0, src ^ 64, :, src] = 1.0
        out[1, src ^ 64, :, 64 + src] = 1.0
        out[2, (127 - src) ^ 64, 0, src] = 1.0
        out[2, (127 - src) ^ 64, 1, src] = -1.0
        out[3, (127 - src) ^ 64, 0, 64 + src] = 1.0
        out[3, (127 - src) ^ 64, 1, 64 + src] = -1.0
    return out.reshape(512, 256).astype(ml_dtypes.bfloat16)


def unfold_matrix():
    out = np.zeros((4, 64, 2, 128), np.float32)
    for row in range(64):
        out[0, row, :, row] = 1.0
        out[1, row, :, 64 + row] = 1.0
        out[2, row, 0, 63 - row] = 1.0
        out[2, row, 1, 63 - row] = -1.0
        out[3, row, 0, 127 - row] = 1.0
        out[3, row, 1, 127 - row] = -1.0
    return out.reshape(256, 256).astype(ml_dtypes.bfloat16)


def scatter_matrix():
    out = np.zeros((2, 2, 5, 8, 128), np.float32)
    for c in range(2):
        for h in range(2):
            for i in range(5):
                for f in range(3):
                    for lev in range(2):
                        out[c, h, i, 2 * f + lev, 40 * f + 4 * (5 * h + i) + 2 * c + lev] = 1.0
    return out.reshape(160, 128).astype(ml_dtypes.bfloat16)


def forward_matrix():
    angle = 2.0 * np.pi * (np.outer(np.arange(64), np.arange(128)) % 128) / 128.0
    table = np.concatenate([np.cos(angle), np.sin(angle)], axis=1) / NLON
    high, low = split_np(table)
    return np.concatenate([high, low], axis=0)


def inverse_matrix():
    angle = 2.0 * np.pi * (np.outer(np.arange(64), np.arange(128)) % 128) / 128.0
    cosine = np.cos(angle).reshape(2, 1, 32, 128)
    sine = np.sin(angle).reshape(2, 1, 32, 128)
    real_part = np.concatenate([cosine, sine], axis=-1)
    imag_part = np.concatenate([-sine, cosine], axis=-1)
    table = np.broadcast_to(np.stack([real_part, imag_part]), (2, 2, 4, 32, 256)).reshape(512, 256)
    high, low = split_np(table)
    return np.concatenate([high, low], axis=0)


def twiddles():
    angle = 2.0 * np.pi * np.outer(np.arange(20), np.arange(128)) / NLON
    return np.stack([np.cos(angle), np.sin(angle)], axis=1).reshape(40, 128).astype(np.float32)


def split(values):
    high = values.astype(BF16)
    return high, (values - high.astype(F32)).astype(BF16)


def dot(left, right):
    return lax.dot_general(left, right, (((1,), (0,)), ((), ())), preferred_element_type=F32)


def dot_t(left, right):
    return lax.dot_general(left, right, (((1,), (1,)), ((), ())), preferred_element_type=F32)


C1, C2 = float(np.cos(2 * np.pi / 5)), float(np.cos(4 * np.pi / 5))
S1, S2 = float(np.sin(2 * np.pi / 5)), float(np.sin(4 * np.pi / 5))


def pack_kernel(
    rank_ref,
    logs_hbm,
    lat_hbm,
    vort_hbm,
    div_hbm,
    height_hbm,
    out0_ref,
    out1_ref,
    out2_ref,
    out3_ref,
    start_ref,
    lat_ref,
    vort_ref,
    div_ref,
    height_ref,
    logs_ref,
    sem_ref,
):
    copies = [
        pltpu.make_async_copy(source, target, sem_ref.at[index])
        for index, (source, target) in enumerate(
            (
                (vort_hbm, vort_ref),
                (div_hbm, div_ref),
                (height_hbm, height_ref),
                (logs_hbm, logs_ref),
                (lat_hbm, lat_ref),
            )
        )
    ]
    for copy in copies:
        copy.start()
    pieces = (out0_ref, out1_ref, out2_ref, out3_ref)
    for piece_ref in pieces:
        piece_ref[pl.ds(60, 4), :] = jnp.zeros((4, 640), F32)
    for copy in copies:
        copy.wait()

    def place(lon):
        for b in range(4):
            for f, ref in enumerate((vort_ref, div_ref, height_ref)):
                for lev in range(2):
                    pieces[(b - lon) % 4][pl.ds((2 * f + lev) * 10, 10), :] = ref[
                        lev, pl.ds(10 * b, 10), :
                    ]

    for lon in range(4):
        pl.when(rank_ref[0] % 4 == lon)(functools.partial(place, lon))

    rank = rank_ref[0]
    first = (rank % 32) * 20 + (rank // 32) * 5
    sub = lax.broadcasted_iota(jnp.int32, (8, LANES), 0)
    for phase in range(2):
        logs = jnp.zeros((8, LANES), F32)
        for slot in range(8):
            offset = min(slot + (635 + 3 * phase if slot >= 5 else 0), 644)
            logs = jnp.where(sub == slot, logs_ref[first + offset], logs)
        start_ref[phase] = logs


def unpack_kernel(
    rank_ref, in0_ref, in1_ref, in2_ref, in3_ref, vort_ref, div_ref, height_ref
):
    pieces = (in0_ref, in1_ref, in2_ref, in3_ref)

    def place(lon):
        for b in range(4):
            for f, ref in enumerate((vort_ref, div_ref, height_ref)):
                for lev in range(2):
                    ref[lev, pl.ds(10 * b, 10), :] = pieces[(lon - b) % 4][
                        pl.ds((2 * f + lev) * 10, 10), :
                    ]

    for lon in range(4):
        pl.when(rank_ref[0] % 4 == lon)(functools.partial(place, lon))


def forward_kernel(
    rank_ref,
    in0_ref,
    in1_ref,
    in2_ref,
    in3_ref,
    twiddle_ref,
    table_ref,
    out_ref,
    z_ref,
    in_ref,
):
    for shift, piece_ref in enumerate((in0_ref, in1_ref, in2_ref, in3_ref)):
        in_ref[(rank_ref[0] + 4 - shift) % 4] = piece_ref[...]

    @pl.loop(0, 8)
    def _(group):
        rows = pl.ds(pl.multiple_of(group * 8, 8), 8)
        x = [in_ref[i2 // 5, rows, pl.ds((i2 % 5) * 128, 128)] for i2 in range(20)]
        parts = []
        for n4 in range(4):
            v = [x[(4 * n5 + 5 * n4) % 20] for n5 in range(5)]
            p1, p2 = v[1] + v[4], v[2] + v[3]
            q1, q2 = v[1] - v[4], v[2] - v[3]
            parts.append(
                (
                    (v[0] + p1 + p2, None),
                    (v[0] + C1 * p1 + C2 * p2, -(S1 * q1 + S2 * q2)),
                    (v[0] + C2 * p1 + C1 * p2, S1 * q2 - S2 * q1),
                )
            )
        y = {}
        zero = jnp.zeros_like(x[0])
        g = [parts[n4][0][0] for n4 in range(4)]
        y[0, 0] = (g[0] + g[2] + (g[1] + g[3]), zero)
        y[2, 0] = (g[0] + g[2] - (g[1] + g[3]), zero)
        y[1, 0] = (g[0] - g[2], g[3] - g[1])
        y[3, 0] = (g[0] - g[2], g[1] - g[3])
        for b5 in (1, 2):
            re = [parts[n4][b5][0] for n4 in range(4)]
            im = [parts[n4][b5][1] for n4 in range(4)]
            er, ei = re[0] + re[2], im[0] + im[2]
            odr, odi = re[1] + re[3], im[1] + im[3]
            dr, di = re[0] - re[2], im[0] - im[2]
            fr, fi = re[1] - re[3], im[1] - im[3]
            y[0, b5] = (er + odr, ei + odi)
            y[2, b5] = (er - odr, ei - odi)
            y[1, b5] = (dr + fi, di - fr)
            y[3, b5] = (dr - fi, di + fr)
        for b in range(20):
            if b % 5 <= 2:
                yr, yi = y[b % 4, b % 5]
            else:
                yr, yi = y[-b % 4, 5 - b % 5]
                yi = -yi
            tr = twiddle_ref[pl.ds(2 * b, 1), :]
            ti = twiddle_ref[pl.ds(2 * b + 1, 1), :]
            z_ref[b, rows, pl.ds(0, 128)] = yr * tr + yi * ti
            z_ref[b, rows, pl.ds(128, 128)] = yi * tr - yr * ti

    table = table_ref[...]
    for b in range(20):
        re = z_ref[b, :, pl.ds(0, 128)]
        im = z_ref[b, :, pl.ds(128, 128)]
        re_hi, re_lo = split(re)
        im_hi, im_lo = split(im)

        def both(real, imag):
            top = jnp.concatenate([real, imag], axis=1)
            return jnp.concatenate([top, jnp.concatenate([imag, -real], axis=1)], axis=0)

        first = dot_t(table, both(re_hi, im_hi))
        total = first[:64] + first[64:] + dot_t(table[:64], both(re_lo, im_lo))
        for h in range(2):
            out_ref[pl.ds((b // 5) * 32, 32), pl.ds((5 * h + b % 5) * 128, 128)] = total[
                h * 32 : (h + 1) * 32
            ]


def inverse_kernel(
    rank_ref,
    in_ref,
    scatter_ref,
    twiddle_ref,
    table_ref,
    out0_ref,
    out1_ref,
    out2_ref,
    out3_ref,
    c_ref,
    z_ref,
    out_ref,
):
    for part in range(4):
        for i in range(5):
            c_ref[part, i, pl.ds(56, 8), :] = jnp.zeros((8, LANES), F32)
    for u in range(10):
        high, low = split(in_ref[:, pl.ds(u * 128, 128)])
        moved = dot_t(scatter_ref[...], high) + dot_t(scatter_ref[...], low)
        for part in range(4):
            for i in range(5):
                start = (part * 5 + i) * 8
                c_ref[part, i, pl.ds(u, 6, stride=10), :] = moved[start : start + 6]
    table_hi = table_ref[pl.ds(0, 512), :]
    table_lo = table_ref[pl.ds(512, 512), :]
    lane_owner = (lax.broadcasted_iota(jnp.int32, (64, 512), 1) % 128) // 32
    for i in range(5):
        block = jnp.concatenate([c_ref[part, i] for part in range(4)], axis=1)
        for b1 in range(4):
            high, low = split(jnp.where(lane_owner == b1, block, 0.0))
            first = dot(jnp.concatenate([high, low], axis=0), table_hi)
            z_ref[5 * b1 + i] = first[:64] + first[64:] + dot(high, table_lo)

    @pl.loop(0, 8)
    def _(group):
        rows = pl.ds(pl.multiple_of(group * 8, 8), 8)
        z = {}
        for b in range(20):
            zr = z_ref[b, rows, pl.ds(0, 128)]
            zi = z_ref[b, rows, pl.ds(128, 128)]
            tr = twiddle_ref[pl.ds(2 * b, 1), :]
            ti = twiddle_ref[pl.ds(2 * b + 1, 1), :]
            z[b % 4, b % 5] = (zr * tr - zi * ti, zr * ti + zi * tr)
        parts = [[None] * 5 for _ in range(4)]
        for b5 in range(5):
            r0, i0 = z[0, b5]
            r1, i1 = z[1, b5]
            r2, i2 = z[2, b5]
            r3, i3 = z[3, b5]
            er, ei, dr, di = r0 + r2, i0 + i2, r0 - r2, i0 - i2
            sr, si, fr, fi = r1 + r3, i1 + i3, r1 - r3, i1 - i3
            parts[0][b5] = (er + sr, ei + si)
            parts[2][b5] = (er - sr, ei - si)
            parts[1][b5] = (dr - fi, di + fr)
            parts[3][b5] = (dr + fi, di - fr)
        for n4 in range(4):
            t = parts[n4]
            base = t[0][0]
            p1, p2 = t[1][0] + t[4][0], t[2][0] + t[3][0]
            q1, q2 = t[1][1] - t[4][1], t[2][1] - t[3][1]
            m1, m2 = base + C1 * p1 + C2 * p2, base + C2 * p1 + C1 * p2
            n1, n2 = S1 * q1 + S2 * q2, S2 * q1 - S1 * q2
            for n5, value in enumerate((base + p1 + p2, m1 - n1, m2 - n2, m2 + n2, m1 + n1)):
                i2 = (4 * n5 + 5 * n4) % 20
                out_ref[i2 // 5, rows, pl.ds((i2 % 5) * 128, 128)] = value

    for shift, piece_ref in enumerate((out0_ref, out1_ref, out2_ref, out3_ref)):
        piece_ref[...] = out_ref[(rank_ref[0] + shift) % 4]


def table_kernel(
    phase,
    rank_ref,
    logs_ref,
    lat_ref,
    before_ref,
    table_ref,
    state_ref,
    coef_ref,
    buf_ref,
    sem_ref,
):
    rank = rank_ref[0]
    first = (rank % 32) * 20 + (rank // 32) * 5
    sub = lax.broadcasted_iota(jnp.int32, (8, LANES), 0)
    lane = lax.broadcasted_iota(jnp.int32, (8, LANES), 1)

    step_index = pl.program_id(0)

    @pl.when(step_index == 0)
    def _():
        fresh = (sub >= 5) | (phase == 0)
        shift = jnp.where(sub >= 5, 635 + 3 * phase, 0)
        wave = (first + sub + shift).astype(F32)
        logs = logs_ref[phase]
        for v in range(TILES):
            lanes = pl.ds(v * LANES, LANES)
            main = wave * lat_ref[pl.ds(1, 1), lanes]
            rest = wave * lat_ref[pl.ds(2, 1), lanes] + logs
            exponent = jnp.floor(main + rest)
            start = -jnp.exp2((main - exponent) + rest)
            state_ref[0, :, lanes] = jnp.where(fresh, 0.0, before_ref[0, :, lanes])
            state_ref[1, :, lanes] = jnp.where(fresh, start, before_ref[1, :, lanes])
            state_ref[2, :, lanes] = jnp.where(fresh, exponent, before_ref[2, :, lanes])

        def coefficients(turn, _):
            block = HALF * phase + turn
            step = block * STEPS + lane
            late = (sub >= 5) & (block >= CHUNKS // 2)
            wave_now = first + sub + jnp.where(sub >= 5, 635, 0) + jnp.where(late, 3, 0)
            excess = step - jnp.where(late, MMAX // 2, 0)
            live = (wave_now + excess < MMAX) & (jnp.logical_not(late) | (sub < 7))
            wave = wave_now.astype(F32)
            k = excess.astype(F32)
            degree = wave + k
            growth = jnp.sqrt((4.0 * degree * degree - 1.0) / jnp.maximum(k * (2.0 * wave + k), 1.0))
            backward = jnp.sqrt(
                jnp.maximum((k - 1.0) * (2.0 * wave + k - 1.0), 0.0)
                / jnp.maximum(4.0 * (degree - 1.0) * (degree - 1.0) - 1.0, 1.0)
            )
            start = excess == 0
            coef_ref[turn, 0] = jnp.where(live & jnp.logical_not(start), growth, 0.0)
            coef_ref[turn, 1] = jnp.where(live, jnp.where(start, 1.0, growth * backward), 0.0)
            return 0

        lax.fori_loop(0, HALF, coefficients, 0)

    slot = step_index % 2

    def copies(step):
        return [
            pltpu.make_async_copy(
                buf_ref.at[step % 2, part // 2, part % 2],
                table_ref.at[step, part // 2, part % 2],
                sem_ref.at[step % 2, part],
            )
            for part in range(4)
        ]

    def finish(step):
        for copy in copies(step):
            copy.wait()

    def generate():
        newer, older, power, scale, cosine = [], [], [], [], []
        for v in range(TILES):
            lanes = pl.ds(v * LANES, LANES)
            newer.append(state_ref[0, :, lanes])
            older.append(state_ref[1, :, lanes])
            power.append(state_ref[2, :, lanes])
            cosine.append(jnp.broadcast_to(lat_ref[pl.ds(0, 1), lanes], (8, LANES)))
            scale.append(jnp.where(power[v] < -126.0, 0.0, jnp.exp2(power[v])))
        growth = coef_ref[step_index, 0]
        backward = coef_ref[step_index, 1]
        held = {}
        for t in range(STEPS):
            a = jnp.broadcast_to(growth[:, t : t + 1], (8, LANES))
            c = jnp.broadcast_to(backward[:, t : t + 1], (8, LANES))
            for v in range(TILES):
                value = (a * cosine[v]) * newer[v] - c * older[v]
                older[v], newer[v] = newer[v], value
                held[t, v] = value * scale[v]
            if t % 8 == 7:
                for v in range(TILES):
                    large = jnp.abs(newer[v]) > renorm_big
                    factor = jnp.where(large, 1.0 / renorm_big, 1.0)
                    newer[v] = newer[v] * factor
                    older[v] = older[v] * factor
                    power[v] = power[v] + jnp.where(large, renorm_step, 0.0)
                    scale[v] = jnp.where(power[v] < -126.0, 0.0, jnp.exp2(power[v]))
            if t % 4 == 3:
                rows = pl.ds((t // 4) * 16, 16)
                for v in range(TILES):
                    lanes = pl.ds(v * LANES, LANES)
                    for parity in range(2):
                        both = jnp.concatenate(
                            [held.pop((t - 3 + parity, v)), held.pop((t - 1 + parity, v))], axis=0
                        )
                        high, low = split(both)
                        buf_ref[slot, parity, 0, rows, lanes] = high
                        buf_ref[slot, parity, 1, rows, lanes] = low
        for v in range(TILES):
            lanes = pl.ds(v * LANES, LANES)
            state_ref[0, :, lanes] = newer[v]
            state_ref[1, :, lanes] = older[v]
            state_ref[2, :, lanes] = power[v]

    pl.when(step_index >= 2)(lambda: finish(step_index - 2))
    generate()
    for copy in copies(step_index):
        copy.start()

    @pl.when(step_index == HALF - 1)
    def _():
        finish(HALF - 2)
        finish(HALF - 1)


def legendre_kernel(
    rank_ref,
    geo_ref,
    in_ref,
    lat_ref,
    gather_ref,
    fold_ref,
    unfold_ref,
    early_ref,
    late_ref,
    out_ref,
    a_ref,
    x_ref,
    update0_ref,
    update1_ref,
    acc_ref,
    table_ref,
    sem_ref,
):
    rank = rank_ref[0]
    first = (rank % 32) * 20 + (rank // 32) * 5
    sub = lax.broadcasted_iota(jnp.int32, (8, LANES), 0)
    lane = lax.broadcasted_iota(jnp.int32, (8, LANES), 1)

    def pieces(source_ref, index, slot):
        return [
            pltpu.make_async_copy(
                source_ref.at[index, part // 2, part % 2],
                table_ref.at[slot, part // 2, part % 2],
                sem_ref.at[slot, part],
            )
            for part in range(4)
        ]

    def fetch(block):
        slot = block % SLOTS

        @pl.when(block < HALF)
        def _():
            for copy in pieces(early_ref, block, slot):
                copy.start()

        @pl.when((block >= HALF) & (block < CHUNKS))
        def _():
            for copy in pieces(late_ref, block - HALF, slot):
                copy.start()

    def arrived(block):
        for copy in pieces(early_ref, 0, block % SLOTS):
            copy.wait()

    for block in range(3):
        fetch(block)

    for u in range(10):
        a_ref[u, pl.ds(120, 8), :] = jnp.zeros((8, LANES), F32)
    for pair in range(5):
        high, low = split(in_ref[:, pl.ds(pair * 256, 256)])
        moved = dot_t(gather_ref[...], high) + dot_t(gather_ref[...], low)
        for u in range(10):
            for f in range(3):
                start = (u * 3 + f) * 8
                a_ref[u, pl.ds(f * 40 + pair * 8, 8), :] = moved[start : start + 8]

    for v in range(TILES):
        lanes = pl.ds(v * LANES, LANES)
        joined = jnp.concatenate(
            [a_ref[2 * v], a_ref[2 * v + 1], a_ref[9 - 2 * v], a_ref[8 - 2 * v]], axis=1
        )
        high, low = split(joined)
        folded = dot(high, fold_ref[...]) + dot(low, fold_ref[...])
        cut = lat_ref[pl.ds(3, 1), lanes]
        weight = lat_ref[pl.ds(4, 1), lanes]
        factors = []
        for pair in range(5):
            q = 2 * pair + sub // 4
            wave = first + q + jnp.where(q >= 5, 635, 0)
            excess = jnp.maximum(wave.astype(F32) - cut, 0.0) / filter_width
            doubling = jnp.where(wave == 0, 1.0, 2.0)
            factors.append(weight * jnp.exp(-0.5 * excess * excess) * doubling)
        factors = jnp.concatenate(factors * 3 + [jnp.zeros((8, LANES), F32)], axis=0)
        for parity in range(2):
            high, low = split(folded[:, parity * LANES : (parity + 1) * LANES] * factors)
            x_ref[parity, pl.ds(0, 128), lanes] = high
            x_ref[parity, pl.ds(128, 128), lanes] = low

    acc_ref[...] = jnp.zeros_like(acc_ref)
    geopot = jnp.where(sub % 2 == 0, geo_ref[0], geo_ref[1])

    def analyse(block, parity, update_ref):
        late = block >= CHUNKS // 2
        slot = lane % 8
        upper = slot >= 5
        wave = first + slot + jnp.where(upper, jnp.where(late, 638 - MMAX // 2, 635), 0)
        owner = slot + jnp.where(upper & late, 3, 0)
        both = dot_t(x_ref[parity], table_ref[block % SLOTS, parity, 0])
        spectral = both[:128] + both[128:] + dot_t(
            x_ref[parity, pl.ds(0, 128), :], table_ref[block % SLOTS, parity, 1]
        )
        halves = []
        for half in range(2):
            step = block * STEPS + 2 * (half * 16 + lane // 8) + parity
            degree = (wave + step).astype(F32)
            ratio = degree * (degree + 1.0) * (1.0 / (MMAX * MMAX))
            coupling = jnp.sqrt(ratio)
            damping = 1.0 / (1.0 + diffusion * ratio * ratio)
            shared = damping / (1.0 + geopot * ratio)
            cross = geopot * coupling
            part = spectral[:, half * LANES : (half + 1) * LANES]
            vort, div, height = [], [], []
            for pair in range(5):
                mine = owner == 2 * pair + sub // 4
                v_part = part[pair * 8 : pair * 8 + 8]
                d_part = part[40 + pair * 8 : 48 + pair * 8]
                h_part = part[80 + pair * 8 : 88 + pair * 8]
                mixed = jnp.where(mine, shared, 0.0)
                vort.append(jnp.where(mine, damping, 0.0) * v_part)
                div.append(mixed * (d_part + coupling * h_part))
                height.append(mixed * (h_part - cross * d_part))
            halves.append(
                jnp.concatenate(vort + div + height + [jnp.zeros((8, LANES), F32)], axis=0)
            )
        high, low = split(jnp.concatenate(halves, axis=1))
        update_ref[parity, pl.ds(0, 128), :] = high
        update_ref[parity, pl.ds(128, 128), :] = low

    def synthesise(block, parity, update_ref):
        both = dot(update_ref[parity], table_ref[block % SLOTS, parity, 0])
        rest = dot(update_ref[parity, pl.ds(0, 128), :], table_ref[block % SLOTS, parity, 1])
        acc_ref[parity] += both[:128] + both[128:] + rest

    arrived(0)
    for parity in range(2):
        analyse(0, parity, update0_ref)

    @pl.loop(0, CHUNKS // 2 - 1)
    def _(pair):
        for turn, (now, later) in enumerate(((update0_ref, update1_ref), (update1_ref, update0_ref))):
            block = 2 * pair + turn
            arrived(block + 1)
            fetch(block + 3)
            for parity in range(2):
                analyse(2 * pair + turn + 1, parity, later)
                synthesise(2 * pair + turn, parity, now)

    arrived(CHUNKS - 1)
    for parity in range(2):
        analyse(CHUNKS - 1, parity, update1_ref)
        synthesise(CHUNKS - 2, parity, update0_ref)
    for parity in range(2):
        synthesise(CHUNKS - 1, parity, update1_ref)

    for v in range(TILES):
        lanes = pl.ds(v * LANES, LANES)
        joined = jnp.concatenate([acc_ref[0, :, lanes], acc_ref[1, :, lanes]], axis=1)
        high, low = split(joined)
        moved = dot_t(unfold_ref[...], high) + dot_t(unfold_ref[...], low)
        for part, u in enumerate((2 * v, 2 * v + 1, 9 - 2 * v, 8 - 2 * v)):
            out_ref[pl.ds(64 - (part // 2) * 64, 64), pl.ds(u * LANES, LANES)] = moved[
                part * 64 : part * 64 + 64
            ]


VMEM = pl.BlockSpec(memory_space=pltpu.VMEM)
SMEM = pl.BlockSpec(memory_space=pltpu.SMEM)
HBM = pl.BlockSpec(memory_space=pltpu.HBM)


def call(kernel, outputs, specs, scratch, megabytes, flops, name, dtype=F32):
    shapes = tuple(jax.ShapeDtypeStruct(shape, dtype) for shape in outputs)
    single = len(shapes) == 1
    return pl.pallas_call(
        kernel,
        out_shape=shapes[0] if single else shapes,
        in_specs=specs,
        out_specs=VMEM if single else tuple(VMEM for _ in shapes),
        scratch_shapes=scratch,
        compiler_params=pltpu.CompilerParams(vmem_limit_bytes=megabytes << 20),
        cost_estimate=pl.CostEstimate(flops=flops, bytes_accessed=2 << 20, transcendentals=0),
        name=name,
    )


def table_call(phase, rank, logs, lat, before):
    def whole(*shape):
        return pl.BlockSpec(shape, lambda step: (0,) * len(shape))

    return pl.pallas_call(
        functools.partial(table_kernel, phase),
        grid=(HALF,),
        out_shape=(
            pltpu.HBM((HALF, 2, 2, 256, 640), BF16),
            jax.ShapeDtypeStruct((3, 8, 640), F32),
        ),
        in_specs=[SMEM, whole(2, 8, LANES), whole(8, 640), whole(3, 8, 640)],
        out_specs=(
            HBM,
            whole(3, 8, 640),
        ),
        scratch_shapes=[
            pltpu.VMEM((HALF, 2, 8, LANES), F32),
            pltpu.VMEM((2, 2, 2, 256, 640), BF16),
            pltpu.SemaphoreType.DMA((2, 4)),
        ],
        compiler_params=pltpu.CompilerParams(vmem_limit_bytes=12 << 20),
        cost_estimate=pl.CostEstimate(flops=1 << 32, bytes_accessed=13 << 20, transcendentals=0),
        name="table",
    )(rank, logs, lat, before)


def exchange(pieces):
    n_lat = lax.axis_size("lat")
    n_lon = lax.axis_size("lon")
    moved = []
    for shift, piece in enumerate(pieces):
        pairs = [
            (lat_at * n_lon + lon_at, (lat_at ^ 16) * n_lon + (lon_at + shift) % n_lon)
            for lat_at in range(n_lat)
            for lon_at in range(n_lon)
        ]
        moved.append(lax.ppermute(piece, ("lat", "lon"), pairs))
    return tuple(moved)


def shards(vorticity, divergence, height, mean_geopot):
    rank = lax.axis_index("lat") * lax.axis_size("lon") + lax.axis_index("lon")
    rank = rank.astype(jnp.int32).reshape(1)
    twiddle = jnp.asarray(twiddles())
    sources = (jnp.asarray(sector_logs()), jnp.asarray(latitude_rows()), vorticity, divergence, height)
    *packed, logs, lat = call(
        pack_kernel,
        [(64, 640)] * 4 + [(2, 8, LANES), (8, 640)],
        [SMEM] + [HBM] * 5,
        [pltpu.VMEM((2, 40, 640), F32) for _ in range(3)]
        + [pltpu.SMEM((MMAX,), F32), pltpu.SemaphoreType.DMA((5,))],
        8,
        1 << 20,
        "pack",
    )(rank, *(pltpu.with_memory_space_constraint(x, pltpu.HBM) for x in sources))
    early, state = table_call(0, rank, logs, lat, jnp.zeros((3, 8, 640), F32))
    sectors = exchange(packed)
    sectors, state = lax.optimization_barrier((sectors, state))
    spectrum = call(
        forward_kernel,
        [(128, 1280)],
        [SMEM] + [VMEM] * 6,
        [pltpu.VMEM((20, 64, 256), F32), pltpu.VMEM((4, 64, 640), F32)],
        16,
        1 << 28,
        "forward",
    )(rank, *sectors, twiddle, jnp.asarray(forward_matrix()))
    spectrum, state = lax.optimization_barrier((spectrum, state))
    late, _ = table_call(1, rank, logs, lat, state)
    columns = lax.all_to_all(spectrum, ("lat", "lon"), split_axis=0, concat_axis=0, tiled=True)
    synthesis = call(
        legendre_kernel,
        [(128, 1280)],
        [SMEM] * 2 + [VMEM] * 5 + [HBM] * 2,
        [
            pltpu.VMEM((10, 128, LANES), F32),
            pltpu.VMEM((2, 256, 640), BF16),
            pltpu.VMEM((2, 256, 256), BF16),
            pltpu.VMEM((2, 256, 256), BF16),
            pltpu.VMEM((2, 128, 640), F32),
            pltpu.VMEM((SLOTS, 2, 2, 256, 640), BF16),
            pltpu.SemaphoreType.DMA((SLOTS, 4)),
        ],
        20,
        1 << 33,
        "legendre",
    )(
        rank,
        mean_geopot,
        columns,
        lat,
        jnp.asarray(gather_matrix()),
        jnp.asarray(fold_matrix()),
        jnp.asarray(unfold_matrix()),
        pltpu.with_memory_space_constraint(early, pltpu.HBM),
        pltpu.with_memory_space_constraint(late, pltpu.HBM),
    )
    gathered = lax.all_to_all(synthesis, ("lat", "lon"), split_axis=0, concat_axis=0, tiled=True)
    result = call(
        inverse_kernel,
        [(64, 640)] * 4,
        [SMEM] + [VMEM] * 4,
        [
            pltpu.VMEM((4, 5, 64, LANES), F32),
            pltpu.VMEM((20, 64, 256), F32),
            pltpu.VMEM((4, 64, 640), F32),
        ],
        16,
        1 << 28,
        "inverse",
    )(rank, gathered, jnp.asarray(scatter_matrix()), twiddle, jnp.asarray(inverse_matrix()))
    pieces = exchange(result)
    return call(unpack_kernel, [(2, 40, 640)] * 3, [SMEM] + [VMEM] * 4, [], 8, 1 << 20, "unpack")(
        rank, *pieces
    )


def solution(mesh):
    placed = (P(None, "lat", "lon"), P(None, "lat", "lon"), P(None, "lat", "lon"), P())
    return jax.shard_map(
        shards,
        mesh=mesh,
        in_specs=placed,
        out_specs=(P(None, "lat", "lon"), P(None, "lat", "lon"), P(None, "lat", "lon")),
        check_vma=False,
    )
```
